128 devices in a mesh: gx: 16 (over y, z), gy: 8 (over x, core).
Axes of the slice: x: 4, y: 4, z: 4, core: 2. Of those that a mesh axis runs over, the one named last changes fastest.
Arguments:
- stream: bfloat16 [256, 18432], P(('gx', 'gy')), may hold values from -6 to 6
- norm_gain: float32 [18432], replicated, may hold values from 0.1 to 1.9
- w_gate: bfloat16 [18432, 36864], P('gx', 'gy'), may hold values from -0.046875 to 0.046875
- w_up: bfloat16 [18432, 36864], P('gx', 'gy'), may hold values from -0.046875 to 0.046875
- w_query: bfloat16 [18432, 6144], P('gx', 'gy'), may hold values from -0.046875 to 0.046875
- w_keyval: bfloat16 [18432, 512], P('gx', 'gy'), may hold values from -0.046875 to 0.046875
- k_cache: bfloat16 [256, 512, 256], P(('gx', 'gy')), may hold values from -200 to 200
- v_cache: bfloat16 [256, 512, 256], P(('gx', 'gy')), may hold values from -6 to 6
- lengths: int32 [256], P(('gx', 'gy')), may hold values from 1 to 512, 65536 in all
Outputs:
- hidden: bfloat16 [256, 36864], P('gx', 'gy')
- context: bfloat16 [256, 6144], P(('gx', 'gy'))
The draws below stay inside these ranges and needn't reach their ends.
Inputs may be any that keep to these rules, and one draw needn't show every extreme that they name: `lengths`: some row has 512 filled slots.
All inputs are finite; a program needn't handle non-finite values. No bound on the sum of `lengths` on one device may be relied on, other than what follows from the above.
Results may differ from the reference program's by a relative error of at most 0.017.
The reference program's roundings to bfloat16 on the way count: a program that leaves them out, or rounds other values in their place, can miss the bound.
Values may be sent and summed in bfloat16 or wider, within the bound.
A program may use at most 128 MiB of HBM per device.

```python
import math
import jax
import jax.numpy as jnp
import numpy as np
from jax import lax

D = 18432
FF = 36864
HEADS = 24
DH = 256
CACHE = 512
B = 256


def draw_k_cache(key, part):
    first = jax.random.fold_in(key, 0)
    base = jax.random.normal(first, (B, CACHE, DH), jnp.float32)
    return jnp.clip(base, -200.0, 200.0).astype(jnp.bfloat16)


def block_levels(own_key, dims, pieces, low, largest):
    def one(dim, shards_of):
        draws = jax.random.uniform(jax.random.fold_in(jax.random.fold_in(own_key, 6), dim), (shards_of,), jnp.float32, low / len(pieces), largest / len(pieces))
        return jnp.repeat(jnp.exp(draws), dims[dim] // shards_of).reshape((-1,) + (1,) * (len(dims) - dim - 1))

    loudness = one(*pieces[0])
    for cut in pieces[1:]:
        loudness = loudness * one(*cut)
    return loudness


def profile(number_of, total, bound, skew):
    portions = [(1 << 20) // math.isqrt(grade ** skew) + 1 for grade in range(2, number_of + 1)]
    rest, given = total - bound - (number_of - 1), [1] * (number_of - 1)
    while rest > 0:
        free = [i for i in range(number_of - 1) if given[i] < bound]
        whole, left = sum([portions[i] for i in free]), rest
        for i in free:
            extra = min(bound - given[i], max(1, left * portions[i] // whole), rest)
            given[i] = given[i] + extra
            rest = rest - extra
    return np.array([bound] + given)


def uneven(key, count, total, reach, slope):
    if count == 2:
        one = jax.random.randint(key, (), max(1, total - reach), min(reach, total - 1) + 1)
        return jnp.stack([one, total - one])
    tallies = jnp.asarray(profile(count, total, reach, slope), jnp.int32)
    couples = (count - 1) // 2
    donor, taker = tallies[1:1 + 2 * couples:2], tallies[2:2 + 2 * couples:2]
    room = jnp.minimum(donor - 1, reach - taker)
    shifted = jax.random.randint(jax.random.fold_in(key, 1), (couples,), 0, 1 << 20) % (room + 1)
    tallies = tallies.at[1:1 + 2 * couples:2].set(donor - shifted).at[2:2 + 2 * couples:2].set(taker + shifted)
    return tallies[jax.random.permutation(jax.random.fold_in(key, 2), count)]


def bell_draw(rng, extent, deviation, bound, shards=(), kind=jnp.bfloat16):
    gain = block_levels(rng, extent, shards, -0.22, 0.18) if shards else 1.0
    array = jax.random.normal(rng, extent, jnp.float32) * deviation * gain
    return jnp.minimum(jnp.maximum(array, -bound), bound).astype(kind)


def setup_inputs(seed: int = 0) -> dict:
    arg_keys = jax.random.split(jax.random.key(seed), 10)
    return {
        "stream": bell_draw(arg_keys[0], (B, D), 1.0, 6.0, ((0, 128),)),
        "norm_gain": jnp.clip(1.0 + 0.18 * jax.random.normal(arg_keys[1], (D,), jnp.float32), 0.1, 1.9),
        "w_gate": bell_draw(arg_keys[2], (D, FF), D ** -0.5, 0.046875, ((0, 16), (1, 8))),
        "w_up": bell_draw(arg_keys[3], (D, FF), D ** -0.5, 0.046875, ((0, 16), (1, 8))),
        "w_query": bell_draw(arg_keys[4], (D, HEADS * DH), D ** -0.5, 0.046875, ((0, 16), (1, 8))),
        "w_keyval": bell_draw(arg_keys[5], (D, 2 * DH), D ** -0.5, 0.046875, ((0, 16), (1, 8))),
        "k_cache": draw_k_cache(jax.random.fold_in(arg_keys[9], 71), 0),
        "v_cache": bell_draw(arg_keys[7], (B, CACHE, DH), 1.0, 6.0, ((0, 128),)),
        "lengths": uneven(arg_keys[8], B, B * CACHE // 2, CACHE, 2).astype(jnp.int32),
    }


def reference(stream, norm_gain, w_gate, w_up, w_query, w_keyval, k_cache, v_cache, lengths):
    values = stream.astype(jnp.float32)
    mean = lax.optimization_barrier(jnp.mean(values, axis=1, keepdims=True))
    centred = values - mean
    variance = lax.optimization_barrier(jnp.mean(centred * centred, axis=1, keepdims=True))
    normed = (centred / jnp.sqrt(variance + 1e-05) * norm_gain[None, :]).astype(jnp.bfloat16)
    gate = jnp.dot(normed, w_gate, preferred_element_type=jnp.float32)
    up_proj = jnp.dot(normed, w_up, preferred_element_type=jnp.float32)
    hidden = (jax.nn.silu(gate) * up_proj).astype(jnp.bfloat16)
    query = jnp.dot(normed, w_query, preferred_element_type=jnp.float32).astype(jnp.bfloat16)
    keyval = jnp.dot(normed, w_keyval, preferred_element_type=jnp.float32).astype(jnp.bfloat16)
    query = query.reshape(B, HEADS, DH).astype(jnp.float32)
    new_key = keyval[:, :DH].astype(jnp.float32)
    new_value = keyval[:, DH:].astype(jnp.float32)
    scale = DH ** (-0.5)
    scores = jnp.einsum('bhd,bld->bhl', query, k_cache.astype(jnp.float32)) * scale
    score_new = jnp.einsum('bhd,bd->bh', query, new_key) * scale
    mask = (jnp.arange(CACHE, dtype=jnp.int32)[None, :] < lengths[:, None])[:, None, :]
    top = jnp.maximum(lax.optimization_barrier(jnp.max(jnp.where(mask, scores, -1e+30), axis=2)), score_new)
    exponent = jnp.where(mask, jnp.exp(scores - top[:, :, None]), 0.0)
    exponent_new = jnp.exp(score_new - top)
    total = lax.optimization_barrier(jnp.sum(exponent, axis=2)) + exponent_new
    weights = (exponent / total[:, :, None]).astype(jnp.bfloat16).astype(jnp.float32)
    weights_new = (exponent_new / total).astype(jnp.bfloat16).astype(jnp.float32)
    context = jnp.einsum('bhl,bld->bhd', weights, v_cache.astype(jnp.float32))
    context = context + weights_new[:, :, None] * new_value[:, None, :]
    return (hidden, context.reshape(B, HEADS * DH).astype(jnp.bfloat16))
```

```python
import jax
import jax.numpy as jnp
from jax import lax
from jax.experimental import pallas as pl
from jax.experimental.pallas import tpu as pltpu
from jax.sharding import PartitionSpec as P

HEADS = 24
DH = 256
D = 18432
K = 1152
FF = 4608
T = 12
W = FF // T
MESH = pl.DeviceIdType.MESH
F32 = jnp.float32
BF16 = jnp.bfloat16


def f32(v):
    return v.astype(F32)


def chunk(ref, axis, i):
    return ref.at[i] if axis == "y" else ref.at[:, i]


class Place:
    def __init__(self):
        gx, self.gy = lax.axis_index("gx"), lax.axis_index("gy")
        self.y, self.z = lax.div(gx, 4), lax.rem(gx, 4)
        self.x, self.c = lax.div(self.gy, 2), lax.rem(self.gy, 2)
        self.gx = gx

    def at(self, axis, k):
        return lax.rem((self.y if axis == "y" else self.z) + (k % 4), 4)

    def dev(self, axis, k):
        if axis == "y":
            return (self.at("y", k) * 4 + self.z, self.gy)
        return (self.y * 4 + self.at("z", k), self.gy)


class Stream:
    def __init__(self, here, first, s, p, far1, rel1, near1, mid, far2, rel2, near2, ss, rs):
        self.here, self.s, self.ss, self.rs = here, s, ss, rs
        self.ax = (first, "z" if first == "y" else "y")
        self.p, self.mid = p, mid
        self.far, self.rel, self.near = (far1, far2), (rel1, rel2), (near1, near2)

    def own(self, ph, k):
        at = self.here.at(self.ax[ph], k)
        return chunk(self.p, self.ax[0], at) if ph == 0 else self.mid.at[at]

    def copy(self, ph, i):
        s = self.s
        src, dst, k = (
            (self.own(ph, 2), self.far[ph], s),
            (self.own(ph, -s), self.near[ph], -s),
            (self.far[ph], self.rel[ph], s),
        )[i]
        return pltpu.make_async_remote_copy(
            src, dst, self.ss.at[ph * 3 + i], self.rs.at[ph * 3 + i],
            device_id=self.here.dev(self.ax[ph], k), device_id_type=MESH,
        )

    def start(self, ph):
        self.copy(ph, 0).start()
        self.copy(ph, 1).start()

    def relay(self, ph):
        self.copy(ph, 0).wait_recv()
        ref = self.far[ph]
        ref[...] = (f32(ref[...]) + f32(self.own(ph, self.s)[...])).astype(ref.dtype)
        self.copy(ph, 2).start()

    def total(self, ph):
        self.copy(ph, 1).wait_recv()
        self.copy(ph, 2).wait_recv()
        return f32(self.own(ph, 0)[...]) + f32(self.rel[ph][...]) + f32(self.near[ph][...])

    def turn(self):
        self.mid[...] = self.total(0).astype(self.mid.dtype)
        self.start(1)

    def drain(self):
        for ph in (0, 1):
            for i in range(3):
                self.copy(ph, i).wait_send()


def kernel(
    stream_h, gain_h, wg_h, wu_h, wq_h, wkv_h,
    hidden, qkv,
    stream, gain, wg, wu, wq, wkv, load_sem, wsem,
    nsend, ybuf, zbuf, a32, xr, perm, xs,
    d_ss, d_rs,
    fp, ff1, fr1, fn1, fm, ff2, fr2, fn2, f_ss, f_rs,
    qp, qf1, qr1, qn1, qm, qf2, qr2, qn2,
    vp, vf1, vr1, vn1, vm, vf2, vr2, vn2, a_ss, a_rs,
    qs, g_ss, g_rs,
):
    h = Place()
    loads = [
        pltpu.make_async_copy(src, dst, load_sem.at[i])
        for i, (src, dst) in enumerate([(stream_h, stream), (gain_h, gain), (wq_h, wq), (wkv_h, wkv)])
    ]
    for c in loads:
        c.start()

    def wload(t):
        cols = pl.ds(pl.multiple_of(t * W, 128), W)
        return (
            pltpu.make_async_copy(wg_h.at[:, cols], wg.at[t], wsem.at[t, 0]),
            pltpu.make_async_copy(wu_h.at[:, cols], wu.at[t], wsem.at[t, 1]),
        )

    @pl.loop(0, T)
    def _(t):
        for c in wload(t):
            c.start()

    bar = pltpu.get_barrier_semaphore()
    for ax in "yz":
        for k in (1, 2, 3):
            pl.semaphore_signal(bar, inc=1, device_id=h.dev(ax, k), device_id_type=MESH)
    for k in range(1, 8):
        pl.semaphore_signal(bar, inc=1, device_id=(h.gx, lax.rem(h.gy + k, 8)), device_id_type=MESH)

    i = lax.broadcasted_iota(jnp.int32, (256, 256), 0)
    j = lax.broadcasted_iota(jnp.int32, (256, 256), 1)
    want = ((i >> 1) & 7) * 32 + (i >> 4) * 2 + (i & 1)
    perm[...] = jnp.where(want == j, 1.0, 0.0).astype(BF16)
    vp[...] = jnp.zeros_like(vp)

    loads[0].wait()
    loads[1].wait()
    total = jnp.zeros((2, K), F32)
    for q in range(16):
        total += f32(stream[:, q * K:(q + 1) * K])
    mean = jnp.sum(total, axis=1, keepdims=True) * (1.0 / D)
    total = jnp.zeros((2, K), F32)
    for q in range(16):
        v = f32(stream[:, q * K:(q + 1) * K]) - mean
        total += v * v
    root = jnp.sqrt(jnp.sum(total, axis=1, keepdims=True) * (1.0 / D) + 1e-05)
    for q in range(16):
        v = (f32(stream[:, q * K:(q + 1) * K]) - mean) / root * gain[:, q * K:(q + 1) * K]
        nsend[q // 4, :, (q % 4) * K:(q % 4 + 1) * K] = v.astype(BF16)

    pl.semaphore_wait(bar, 13)

    first = [
        pltpu.make_async_remote_copy(
            nsend.at[h.at("y", k)], ybuf.at[h.y], d_ss.at[k], d_rs.at[k],
            device_id=h.dev("y", k), device_id_type=MESH)
        for k in (2, 1, 3)
    ]
    for c in first:
        c.start()
    ybuf[h.y] = nsend[h.y]
    for c in first:
        c.wait_recv()

    def zcols(zd):
        return pl.ds(pl.multiple_of(zd * K, 128), K)

    second = [
        pltpu.make_async_remote_copy(
            ybuf.at[:, :, zcols(h.at("z", k))], zbuf.at[h.z], d_ss.at[3 + k], d_rs.at[3 + k],
            device_id=h.dev("z", k), device_id_type=MESH)
        for k in (2, 1, 3)
    ]
    for c in second:
        c.start()
    zbuf[h.z] = ybuf[:, :, zcols(h.z)]
    for c in second:
        c.wait_recv()
    for y in range(4):
        for z in range(4):
            r = (y * 4 + z) * 2
            a32[r:r + 2, :] = f32(zbuf[z, y])
    xr[h.gy] = a32[...].astype(BF16)

    def to_x(k):
        return pltpu.make_async_remote_copy(
            xr.at[h.gy], xr.at[h.gy], d_ss.at[7 + k], d_rs.at[7 + k],
            device_id=(h.gx, lax.rem(h.gy + 2 * k, 8)), device_id_type=MESH)

    def to_partner(k):
        g = lax.rem(h.gy + 8 - 2 * k, 8)
        return pltpu.make_async_remote_copy(
            xr.at[g], xr.at[g], d_ss.at[11 + k], d_rs.at[11 + k],
            device_id=(h.gx, h.x * 2 + 1 - h.c), device_id_type=MESH)

    third = [to_x(k) for k in (2, 1, 3)]
    for c in third:
        c.start()
    fourth = [to_partner(k) for k in range(4)]
    fourth[0].start()
    for k in (1, 3, 2):
        to_x(k).wait_recv()
        fourth[k].start()
    for c in fourth:
        c.wait_recv()
    for n in range(3):
        cols = slice(n * 384, (n + 1) * 384)
        xs[:, cols] = jnp.dot(
            perm[...], xr[:, :, cols].reshape(256, 384), preferred_element_type=F32
        ).astype(BF16)
    for c in first + second + third + fourth:
        c.wait_send()

    att = [
        Stream(h, first, s, qp.at[n], qf1.at[n], qr1.at[n], qn1.at[n], qm.at[n], qf2.at[n], qr2.at[n], qn2.at[n],
               a_ss.at[n], a_rs.at[n])
        for n, (first, s) in enumerate([("y", -1), ("z", 1), ("y", 1)])
    ]
    att.append(Stream(h, "z", -1, vp, vf1, vr1, vn1, vm, vf2, vr2, vn2, a_ss.at[3], a_rs.at[3]))

    def ffn(t, n, order):
        return Stream(h, order, -1 if n == 0 else 1, fp.at[t, n], ff1.at[t, n], fr1.at[t, n], fn1.at[t, n],
                      fm.at[t, n], ff2.at[t, n], fr2.at[t, n], fn2.at[t, n], f_ss.at[t, n], f_rs.at[t, n])

    def pair(i, do):
        for t, order in ((2 * i, "y"), (2 * i + 1, "z")):
            do(t, [ffn(t, n, order) for n in (0, 1)])

    loads[2].wait()
    loads[3].wait()
    for n in range(3):
        qp[n] = jnp.dot(xs[...], wq[:, n * DH:(n + 1) * DH], preferred_element_type=F32).reshape(4, 4, 16, DH)
        att[n].start(0)
    vp[:, :, :, 0:64] = jnp.dot(xs[...], wkv[...], preferred_element_type=F32).reshape(4, 4, 16, 64)
    att[3].start(0)

    def compute(t, streams):
        for c in wload(t):
            c.wait()
        for n, w in ((0, wg), (1, wu)):
            fp[t, n] = jnp.dot(xs[...], w[t], preferred_element_type=F32).astype(BF16).reshape(4, 4, 16, W)
            streams[n].start(0)

    def computes(lo, hi):
        @pl.loop(lo, hi)
        def _(i):
            pair(i, compute)

    computes(0, 2)
    for s in att:
        s.relay(0)
    computes(2, 3)
    for s in att:
        s.turn()
    computes(3, 4)
    for s in att:
        s.relay(1)
    computes(4, T // 2)

    @pl.loop(0, T // 2)
    def _(i):
        pair(i, lambda t, ss: [s.relay(0) for s in ss])

    for n, s in enumerate(att):
        val = s.total(1)
        for g in range(8):
            qs[g, :, n * DH:n * DH + val.shape[1]] = val[2 * g:2 * g + 2, :].astype(BF16)
    give = [
        pltpu.make_async_remote_copy(
            qs.at[lax.rem(h.gy + k, 8)], qkv.at[h.gy], g_ss.at[k], g_rs.at[k],
            device_id=(h.gx, lax.rem(h.gy + k, 8)), device_id_type=MESH)
        for k in range(1, 8)
    ]
    for c in give:
        c.start()
    qkv[h.gy] = qs[h.gy]

    @pl.loop(0, T // 2)
    def _(i):
        pair(i, lambda t, ss: [s.turn() for s in ss])

    @pl.loop(0, T // 2)
    def _(i):
        pair(i, lambda t, ss: [s.relay(1) for s in ss])

    def finish(t, ss):
        gate, up = ss[0].total(1), ss[1].total(1)
        cols = pl.ds(pl.multiple_of(t * W, 128), W)
        hidden[:, cols] = (gate / (1.0 + jnp.exp(-gate)) * up).astype(BF16)

    @pl.loop(0, T // 2)
    def _(i):
        pair(i, finish)

    for c in give:
        c.wait()
    for s in att:
        s.drain()

    @pl.loop(0, T // 2)
    def _(i):
        pair(i, lambda t, ss: [s.drain() for s in ss])


def fused(stream, gain, w_gate, w_up, w_query, w_keyval):
    vm, dma = pltpu.VMEM, pltpu.SemaphoreType.DMA

    def rs(lead, wide, kind):
        return [
            vm(lead + (4, 4, 16, wide), kind),
            *[vm(lead + (4, 16, wide), kind)] * 3,
            vm(lead + (4, 16, wide), kind),
            *[vm(lead + (16, wide), kind)] * 3,
        ]

    return pl.pallas_call(
        kernel,
        out_shape=(
            jax.ShapeDtypeStruct((16, FF), BF16),
            jax.ShapeDtypeStruct((8, 2, 896), BF16),
        ),
        in_specs=[pl.BlockSpec(memory_space=pl.ANY)] * 6,
        out_specs=[pl.BlockSpec(memory_space=pltpu.VMEM)] * 2,
        scratch_shapes=[
            vm((2, D), BF16), vm((1, D), F32), vm((T, K, W), BF16), vm((T, K, W), BF16),
            vm((K, 768), BF16), vm((K, 64), BF16), dma((4,)), dma((T, 2)),
            vm((4, 2, 4 * K), BF16), vm((4, 2, 4 * K), BF16), vm((4, 4, 2, K), BF16), vm((32, K), F32),
            vm((8, 32, K), BF16), vm((256, 256), BF16), vm((256, K), BF16),
            dma((15,)), dma((15,)),
            *rs((T, 2), W, BF16), dma((T, 2, 6)), dma((T, 2, 6)),
            *rs((3,), DH, F32),
            *rs((), 128, F32), dma((4, 6)), dma((4, 6)),
            vm((8, 2, 896), BF16), dma((8,)), dma((8,)),
        ],
        compiler_params=pltpu.CompilerParams(
            collective_id=0, has_side_effects=True, vmem_limit_bytes=62 * 2**20
        ),
    )(stream, gain, w_gate, w_up, w_query, w_keyval)


def body(stream, norm_gain, w_gate, w_up, w_query, w_keyval, k_cache, v_cache, lengths):
    hidden, pieces = fused(stream, norm_gain.reshape(1, D), w_gate, w_up, w_query, w_keyval)
    rows = 2
    pieces = jnp.swapaxes(pieces, 0, 1)
    query = pieces[:, :, :768].reshape(rows, HEADS, DH)
    keyval = pieces[:, :, 768:832].reshape(rows, 512)
    new_key = keyval[:, :DH]
    new_value = keyval[:, DH:]
    scale = DH ** (-0.5)
    scores = jnp.einsum("bhd,bld->bhl", query, k_cache, preferred_element_type=F32) * scale
    score_new = jnp.einsum("bhd,bd->bh", query, new_key, preferred_element_type=F32) * scale
    mask = (jnp.arange(k_cache.shape[1], dtype=jnp.int32)[None, :] < lengths[:, None])[:, None, :]
    top = jnp.maximum(jnp.max(jnp.where(mask, scores, -1e30), axis=2), score_new)
    exponent = jnp.where(mask, jnp.exp(scores - top[:, :, None]), 0.0)
    exponent_new = jnp.exp(score_new - top)
    total = jnp.sum(exponent, axis=2) + exponent_new
    weights = (exponent / total[:, :, None]).astype(BF16)
    weights_new = (exponent_new / total).astype(BF16)
    context = jnp.einsum("bhl,bld->bhd", weights, v_cache, preferred_element_type=F32)
    context = context + f32(weights_new)[:, :, None] * f32(new_value)[:, None, :]
    return (hidden, context.reshape(rows, HEADS * DH).astype(BF16))


def solution(mesh):
    return jax.shard_map(
        body,
        mesh=mesh,
        in_specs=(
            P(("gx", "gy"), None),
            P(),
            P("gx", "gy"),
            P("gx", "gy"),
            P("gx", "gy"),
            P("gx", "gy"),
            P(("gx", "gy"), None, None),
            P(("gx", "gy"), None, None),
            P(("gx", "gy")),
        ),
        out_specs=(P("gx", "gy"), P(("gx", "gy"), None)),
        check_vma=False,
    )
```

```python
import functools

import jax
import jax.numpy as jnp
from jax import lax
from jax.experimental import pallas as pl
from jax.experimental.pallas import tpu as pltpu
from jax.sharding import PartitionSpec as P

HEADS = 24
DH = 256
D = 18432
K = 1152
FF = 4608
T = 12
DIRECT = 4
CACHE = 512
W = FF // T
MESH = pl.DeviceIdType.MESH
F32 = jnp.float32
BF16 = jnp.bfloat16


def f32(v):
    return v.astype(F32)


def chunk(ref, axis, i):
    return ref.at[i] if axis == "y" else ref.at[:, i]


class Place:
    def __init__(self):
        gx, self.gy = lax.axis_index("gx"), lax.axis_index("gy")
        self.y, self.z = lax.div(gx, 4), lax.rem(gx, 4)
        self.x, self.c = lax.div(self.gy, 2), lax.rem(self.gy, 2)
        self.gx = gx

    def at(self, axis, k):
        return lax.rem((self.y if axis == "y" else self.z) + (k % 4), 4)

    def dev(self, axis, k):
        if axis == "y":
            return (self.at("y", k) * 4 + self.z, self.gy)
        return (self.y * 4 + self.at("z", k), self.gy)


class Stream:
    def __init__(self, here, first, s, p, far1, rel1, near1, mid, far2, rel2, near2, ss, rs):
        self.here, self.s, self.ss, self.rs = here, s, ss, rs
        self.ax = (first, "z" if first == "y" else "y")
        self.p, self.mid = p, mid
        self.far, self.rel, self.near = (far1, far2), (rel1, rel2), (near1, near2)

    def own(self, ph, k):
        at = self.here.at(self.ax[ph], k)
        return chunk(self.p, self.ax[0], at) if ph == 0 else self.mid.at[at]

    def copy(self, ph, i, direct=False):
        s = self.s
        src, dst, k = (
            (self.own(ph, 2), self.far[ph], 2 if direct else s),
            (self.own(ph, -s), self.near[ph], -s),
            (self.own(ph, s) if direct else self.far[ph], self.rel[ph], s),
        )[i]
        return pltpu.make_async_remote_copy(
            src, dst, self.ss.at[ph * 3 + i], self.rs.at[ph * 3 + i],
            device_id=self.here.dev(self.ax[ph], k), device_id_type=MESH,
        )

    def start(self, ph, direct=False):
        self.copy(ph, 0, direct).start()
        self.copy(ph, 1).start()
        if direct:
            self.copy(ph, 2, direct).start()

    def relay(self, ph):
        self.copy(ph, 0).wait_recv()
        ref = self.far[ph]
        ref[...] = (f32(ref[...]) + f32(self.own(ph, self.s)[...])).astype(ref.dtype)
        self.copy(ph, 2).start()

    def total(self, ph, direct=False):
        value = f32(self.own(ph, 0)[...])
        if direct:
            self.copy(ph, 0, direct).wait_recv()
            value += f32(self.far[ph][...])
        self.copy(ph, 1).wait_recv()
        self.copy(ph, 2, direct).wait_recv()
        return value + f32(self.rel[ph][...]) + f32(self.near[ph][...])

    def turn(self, direct=False):
        self.mid[...] = self.total(0).astype(self.mid.dtype)
        self.start(1, direct)

    def drain(self):
        for ph in (0, 1):
            for i in range(3):
                self.copy(ph, i).wait_send()


def kernel(
    stream_h, gain_h, wg_h, wu_h, wq_h, wkv_h, k_h, v_h, lengths,
    hidden, context,
    stream, gain, wg, wu, wq, wkv, kc, vc, load_sem, wsem,
    nsend, ybuf, zbuf, a8, xr, perm, xs,
    d_ss, d_rs, x_ss, x_rs, p_ss, p_rs,
    fp, ff1, fr1, fn1, fm, ff2, fr2, fn2, f_ss, f_rs,
    qp, qf1, qr1, qn1, qm, qf2, qr2, qn2,
    vp, vf1, vr1, vn1, vm, vf2, vr2, vn2, a_ss, a_rs,
    qs, qr, qa, kvs, g_ss, g_rs,
):
    h = Place()
    loads = [
        pltpu.make_async_copy(src, dst, load_sem.at[i])
        for i, (src, dst) in enumerate([(stream_h, stream), (gain_h, gain), (wq_h, wq), (wkv_h, wkv), (k_h, kc), (v_h, vc)])
    ]
    for c in loads[:4]:
        c.start()

    def wload(t):
        cols = pl.ds(pl.multiple_of(t * W, 128), W)
        return (
            pltpu.make_async_copy(wg_h.at[:, cols], wg.at[t], wsem.at[t, 0]),
            pltpu.make_async_copy(wu_h.at[:, cols], wu.at[t], wsem.at[t, 1]),
        )

    @pl.loop(0, T)
    def _(t):
        for c in wload(t):
            c.start()

    for c in loads[4:]:
        c.start()

    bar = pltpu.get_barrier_semaphore()
    for ax in "yz":
        for k in (1, 2, 3):
            pl.semaphore_signal(bar, inc=1, device_id=h.dev(ax, k), device_id_type=MESH)
    for k in range(1, 8):
        pl.semaphore_signal(bar, inc=1, device_id=(h.gx, lax.rem(h.gy + k, 8)), device_id_type=MESH)

    i = lax.broadcasted_iota(jnp.int32, (256, 256), 0)
    j = lax.broadcasted_iota(jnp.int32, (256, 256), 1)
    want = ((i >> 1) & 7) * 32 + ((i >> 4) & 3) * 8 + (i >> 6) * 2 + (i & 1)
    perm[...] = jnp.where(want == j, 1.0, 0.0).astype(BF16)
    vp[...] = jnp.zeros_like(vp)

    loads[0].wait()
    loads[1].wait()
    total = jnp.zeros((2, K), F32)
    for q in range(16):
        total += f32(stream[:, q * K:(q + 1) * K])
    mean = jnp.sum(total, axis=1, keepdims=True) * (1.0 / D)
    total = jnp.zeros((2, K), F32)
    for q in range(16):
        v = f32(stream[:, q * K:(q + 1) * K]) - mean
        total += v * v
    root = jnp.sqrt(jnp.sum(total, axis=1, keepdims=True) * (1.0 / D) + 1e-05)
    for q in range(16):
        v = (f32(stream[:, q * K:(q + 1) * K]) - mean) / root * gain[:, q * K:(q + 1) * K]
        nsend[q // 4, :, (q % 4) * K:(q % 4 + 1) * K] = v.astype(BF16)

    pl.semaphore_wait(bar, 13)

    first = [
        pltpu.make_async_remote_copy(
            nsend.at[h.at("y", k)], ybuf.at[h.y], d_ss.at[k], d_rs.at[k],
            device_id=h.dev("y", k), device_id_type=MESH)
        for k in (2, 1, 3)
    ]
    for c in first:
        c.start()
    ybuf[h.y] = nsend[h.y]
    for c in first:
        c.wait_recv()

    def zcols(zd):
        return pl.ds(pl.multiple_of(zd * K, 128), K)

    second = [
        pltpu.make_async_remote_copy(
            ybuf.at[:, :, zcols(h.at("z", k))], zbuf.at[h.z], d_ss.at[3 + k], d_rs.at[3 + k],
            device_id=h.dev("z", k), device_id_type=MESH)
        for k in (2, 1, 3)
    ]
    for c in second:
        c.start()

    def along(k):
        return lax.rem(h.gy + 2 * k, 8)

    def remote(src, dst, ss, rs, gy):
        return pltpu.make_async_remote_copy(
            src, dst, ss, rs, device_id=(h.gx, gy), device_id_type=MESH)

    def to_x(n, k):
        z = h.at("z", n)
        return remote(xr.at[h.gy, z], xr.at[h.gy, z], x_ss.at[n, k - 1], x_rs.at[n, k - 1], along(k))

    def to_partner(n, k):
        g, z = along(4 - k), h.at("z", n)
        return remote(xr.at[g, z], xr.at[g, z], p_ss.at[n, k], p_rs.at[n, k], h.x * 2 + 1 - h.c)

    for n in (0, 1, 3, 2):
        z = h.at("z", n)
        if n == 0:
            for y in range(4):
                a8[n, 2 * y:2 * y + 2, :] = f32(ybuf[y, :, zcols(h.z)])
        else:
            second[{2: 0, 1: 1, 3: 2}[4 - n]].wait_recv()
            for y in range(4):
                a8[n, 2 * y:2 * y + 2, :] = f32(zbuf[z, y])
        xr[h.gy, z] = a8[n].astype(BF16)
        for k in (2, 1, 3):
            to_x(n, k).start()
        to_partner(n, 0).start()
    for n in (0, 1, 3, 2):
        for k in (1, 3, 2):
            to_x(n, k).wait_recv()
            to_partner(n, k).start()
    for n in (0, 1, 3, 2):
        for k in range(4):
            to_partner(n, k).wait_recv()
    for n in range(3):
        cols = slice(n * 384, (n + 1) * 384)
        xs[:, cols] = jnp.dot(
            perm[...], xr[:, :, :, cols].reshape(256, 384), preferred_element_type=F32
        ).astype(BF16)
    for c in first + second:
        c.wait_send()
    for n in range(4):
        for k in (1, 2, 3):
            to_x(n, k).wait_send()
        for k in range(4):
            to_partner(n, k).wait_send()

    att = [
        Stream(h, first, s, qp.at[n], qf1.at[n], qr1.at[n], qn1.at[n], qm.at[n], qf2.at[n], qr2.at[n], qn2.at[n],
               a_ss.at[n], a_rs.at[n])
        for n, (first, s) in enumerate([("y", -1), ("z", 1), ("y", 1)])
    ]
    att.append(Stream(h, "z", -1, vp, vf1, vr1, vn1, vm, vf2, vr2, vn2, a_ss.at[3], a_rs.at[3]))

    def ffn(t, n, order):
        return Stream(h, order, -1 if n == 0 else 1, fp.at[t, n], ff1.at[t, n], fr1.at[t, n], fn1.at[t, n],
                      fm.at[t, n], ff2.at[t, n], fr2.at[t, n], fn2.at[t, n], f_ss.at[t, n], f_rs.at[t, n])

    def pair(i, do):
        for t, order in ((2 * i, "y"), (2 * i + 1, "z")):
            do(t, [ffn(t, n, order) for n in (0, 1)])

    loads[2].wait()
    loads[3].wait()
    query = jnp.dot(xs[...], wq[...], preferred_element_type=F32)
    for n in range(3):
        qp[n] = query[:, n * DH:(n + 1) * DH].reshape(4, 4, 16, DH)
    vp[:, :, :, 0:64] = lax.dot_general(
        xs[...], wkv[...], (((1,), (1,)), ((), ())), preferred_element_type=F32
    ).reshape(4, 4, 16, 64)
    for s in att:
        s.start(0)

    def computes(lo, hi):
        @pl.loop(lo, hi)
        def _(i):
            pair(i, lambda t, ss: [c.wait() for c in wload(t)])
            for t in (2 * i, 2 * i + 1):
                for n, w in ((0, wg), (1, wu)):
                    fp[t, n] = jnp.dot(xs[...], w[t], preferred_element_type=F32).astype(BF16).reshape(4, 4, 16, W)
            pair(i, lambda t, ss: [s.start(0) for s in ss])

    def each(lo, hi, do):
        @pl.loop(lo, hi)
        def _(i):
            pair(i, lambda t, ss: [do(s) for s in ss])

    computes(0, 2)
    for s in att:
        s.relay(0)
    computes(2, T // 2)
    for s in att:
        s.turn(True)
    each(0, T // 2, lambda s: s.relay(0))
    each(0, DIRECT, lambda s: s.turn())
    each(DIRECT, T // 2, lambda s: s.turn(True))

    for n, s in enumerate(att):
        val = s.total(1, True)
        for g in range(8):
            qs[g, :, n * DH:n * DH + val.shape[1]] = val[2 * g:2 * g + 2, :].astype(BF16)
    give = [
        pltpu.make_async_remote_copy(
            qs.at[lax.rem(h.gy + k, 8)], qr.at[h.gy], g_ss.at[k], g_rs.at[k],
            device_id=(h.gx, lax.rem(h.gy + k, 8)), device_id_type=MESH)
        for k in range(1, 8)
    ]
    for c in give:
        c.start()
    qr[h.gy] = qs[h.gy]

    each(0, DIRECT, lambda s: s.relay(1))

    for c in give:
        c.wait_recv()
    for g in range(8):
        for n in range(3):
            row = f32(qr[g, :, n * DH:(n + 1) * DH])
            for r in range(2):
                qa[r, g * 3 + n:g * 3 + n + 1, :] = row[r:r + 1, :]
        kvs[2 * g:2 * g + 2, :] = f32(qr[g, :, 768:896])
    moved = pltpu.roll(kvs[...], 64, axis=1)

    def whole(r, first):
        row = [(kvs[2 * g + r:2 * g + r + 1, :], moved[2 * g + r:2 * g + r + 1, :]) for g in range(first, first + 4)]
        return jnp.concatenate([row[0][0] + row[1][1], row[2][0] + row[3][1]], axis=1)

    loads[4].wait()
    loads[5].wait()
    scale = DH ** (-0.5)
    for r in range(2):
        query = qa[r]
        scores = lax.dot_general(
            query.astype(BF16), kc[r], (((1,), (1,)), ((), ())), preferred_element_type=F32) * scale
        score_new = jnp.sum(query * whole(r, 0), axis=1, keepdims=True) * scale
        mask = lax.broadcasted_iota(jnp.int32, (HEADS, CACHE), 1) < lengths[r]
        top = jnp.maximum(jnp.max(jnp.where(mask, scores, -1e30), axis=1, keepdims=True), score_new)
        exponent = jnp.where(mask, jnp.exp(scores - top), 0.0)
        exponent_new = jnp.exp(score_new - top)
        total = jnp.sum(exponent, axis=1, keepdims=True) + exponent_new
        weights = (exponent / total).astype(BF16)
        weights_new = f32((exponent_new / total).astype(BF16))
        out = jnp.dot(weights, vc[r], preferred_element_type=F32) + weights_new * whole(r, 4)
        context[r] = out.astype(BF16)

    def finish(direct, t, ss):
        gate, up = ss[0].total(1, direct), ss[1].total(1, direct)
        cols = pl.ds(pl.multiple_of(t * W, 128), W)
        hidden[:, cols] = (gate / (1.0 + jnp.exp(-gate)) * up).astype(BF16)

    @pl.loop(0, DIRECT)
    def _(i):
        pair(i, functools.partial(finish, False))

    @pl.loop(DIRECT, T // 2)
    def _(i):
        pair(i, functools.partial(finish, True))

    for c in give:
        c.wait_send()
    for s in att:
        s.drain()

    each(0, T // 2, lambda s: s.drain())


def fused(stream, gain, w_gate, w_up, w_query, w_keyval, k_cache, v_cache, lengths):
    vm, dma = pltpu.VMEM, pltpu.SemaphoreType.DMA

    def rs(lead, wide, kind):
        return [
            vm(lead + (4, 4, 16, wide), kind),
            *[vm(lead + (4, 16, wide), kind)] * 3,
            vm(lead + (4, 16, wide), kind),
            *[vm(lead + (16, wide), kind)] * 3,
        ]

    return pl.pallas_call(
        kernel,
        out_shape=(
            jax.ShapeDtypeStruct((16, FF), BF16),
            jax.ShapeDtypeStruct((2, HEADS, DH), BF16),
        ),
        in_specs=[pl.BlockSpec(memory_space=pl.ANY)] * 8 + [pl.BlockSpec(memory_space=pltpu.SMEM)],
        out_specs=[pl.BlockSpec(memory_space=pltpu.VMEM)] * 2,
        scratch_shapes=[
            vm((2, D), BF16), vm((1, D), F32), vm((T, K, W), BF16), vm((T, K, W), BF16),
            vm((K, 768), BF16), vm((64, K), BF16), vm((2, CACHE, DH), BF16), vm((2, CACHE, DH), BF16),
            dma((6,)), dma((T, 2)),
            vm((4, 2, 4 * K), BF16), vm((4, 2, 4 * K), BF16), vm((4, 4, 2, K), BF16), vm((4, 8, K), F32),
            vm((8, 4, 8, K), BF16), vm((256, 256), BF16), vm((256, K), BF16),
            dma((7,)), dma((7,)), dma((4, 3)), dma((4, 3)), dma((4, 4)), dma((4, 4)),
            *rs((T, 2), W, BF16), dma((T, 2, 6)), dma((T, 2, 6)),
            *rs((3,), DH, F32),
            *rs((), 128, F32), dma((4, 6)), dma((4, 6)),
            vm((8, 2, 896), BF16), vm((8, 2, 896), BF16), vm((2, HEADS, DH), F32), vm((16, 128), F32),
            dma((8,)), dma((8,)),
        ],
        compiler_params=pltpu.CompilerParams(
            collective_id=0, has_side_effects=True, vmem_limit_bytes=62 * 2**20
        ),
    )(stream, gain, w_gate, w_up, w_query, w_keyval, k_cache, v_cache, lengths)


def body(stream, norm_gain, w_gate, w_up, w_query, w_keyval, k_cache, v_cache, lengths):
    hidden, context = fused(
        stream, norm_gain.reshape(1, D), w_gate, w_up, w_query, w_keyval.T, k_cache, v_cache, lengths
    )
    return (hidden, context.reshape(2, HEADS * DH))


def solution(mesh):
    return jax.shard_map(
        body,
        mesh=mesh,
        in_specs=(
            P(("gx", "gy"), None),
            P(),
            P("gx", "gy"),
            P("gx", "gy"),
            P("gx", "gy"),
            P("gx", "gy"),
            P(("gx", "gy"), None, None),
            P(("gx", "gy"), None, None),
            P(("gx", "gy")),
        ),
        out_specs=(P("gx", "gy"), P(("gx", "gy"), None)),
        check_vma=False,
    )
```

```python
import functools

import jax
import jax.numpy as jnp
from jax import lax
from jax.experimental import pallas as pl
from jax.experimental.pallas import tpu as pltpu
from jax.sharding import PartitionSpec as P

HEADS = 24
DH = 256
D = 18432
K = 1152
FF = 4608
T = 12
DIRECT = 4
CACHE = 512
W = FF // T
MESH = pl.DeviceIdType.MESH
F32 = jnp.float32
BF16 = jnp.bfloat16


def f32(v):
    return v.astype(F32)


def chunk(ref, axis, i):
    return ref.at[i] if axis == "y" else ref.at[:, i]


class Place:
    def __init__(self):
        gx, self.gy = lax.axis_index("gx"), lax.axis_index("gy")
        self.y, self.z = lax.div(gx, 4), lax.rem(gx, 4)
        self.x, self.c = lax.div(self.gy, 2), lax.rem(self.gy, 2)
        self.gx = gx

    def at(self, axis, k):
        return lax.rem((self.y if axis == "y" else self.z) + (k % 4), 4)

    def dev(self, axis, k):
        if axis == "y":
            return (self.at("y", k) * 4 + self.z, self.gy)
        return (self.y * 4 + self.at("z", k), self.gy)


class Stream:
    def __init__(self, here, first, s, p, far1, rel1, near1, mid, far2, rel2, near2, ss, rs):
        self.here, self.s, self.ss, self.rs = here, s, ss, rs
        self.ax = (first, "z" if first == "y" else "y")
        self.p, self.mid = p, mid
        self.far, self.rel, self.near = (far1, far2), (rel1, rel2), (near1, near2)

    def own(self, ph, k):
        at = self.here.at(self.ax[ph], k)
        return chunk(self.p, self.ax[0], at) if ph == 0 else self.mid.at[at]

    def copy(self, ph, i, direct=False):
        s = self.s
        src, dst, k = (
            (self.own(ph, 2), self.far[ph], 2 if direct else s),
            (self.own(ph, -s), self.near[ph], -s),
            (self.own(ph, s) if direct else self.far[ph], self.rel[ph], s),
        )[i]
        return pltpu.make_async_remote_copy(
            src, dst, self.ss.at[ph * 3 + i], self.rs.at[ph * 3 + i],
            device_id=self.here.dev(self.ax[ph], k), device_id_type=MESH,
        )

    def start(self, ph, direct=False):
        self.copy(ph, 0, direct).start()
        self.copy(ph, 1).start()
        if direct:
            self.copy(ph, 2, direct).start()

    def relay(self, ph):
        self.copy(ph, 0).wait_recv()
        ref = self.far[ph]
        ref[...] = (f32(ref[...]) + f32(self.own(ph, self.s)[...])).astype(ref.dtype)
        self.copy(ph, 2).start()

    def total(self, ph, direct=False):
        value = f32(self.own(ph, 0)[...])
        if direct:
            self.copy(ph, 0, direct).wait_recv()
            value += f32(self.far[ph][...])
        self.copy(ph, 1).wait_recv()
        self.copy(ph, 2, direct).wait_recv()
        return value + f32(self.rel[ph][...]) + f32(self.near[ph][...])

    def turn(self, direct=False):
        self.mid[...] = self.total(0).astype(self.mid.dtype)
        self.start(1, direct)

    def drain(self):
        for ph in (0, 1):
            for i in range(3):
                self.copy(ph, i).wait_send()


def kernel(
    stream_h, gain_h, wg_h, wu_h, wq_h, wkv_h, k_h, v_h, lengths_h,
    hidden, context,
    stream, gain, wg, wu, wq, wkv, kc, vc, lengths, load_sem, wsem,
    nsend, ybuf, zbuf, a8, xr, perm, xs,
    d_ss, d_rs, x_ss, x_rs, p_ss, p_rs,
    fp, ff1, fr1, fn1, fm, ff2, fr2, fn2, f_ss, f_rs,
    qp, qf1, qr1, qn1, qm, qf2, qr2, qn2,
    vp, vf1, vr1, vn1, vm, vf2, vr2, vn2, a_ss, a_rs,
    qs, qr, qa, kvs, g_ss, g_rs,
):
    h = Place()
    bar = pltpu.get_barrier_semaphore()
    for ax in "yz":
        for k in (1, 2, 3):
            pl.semaphore_signal(bar, inc=1, device_id=h.dev(ax, k), device_id_type=MESH)
    for k in range(1, 8):
        pl.semaphore_signal(bar, inc=1, device_id=(h.gx, lax.rem(h.gy + k, 8)), device_id_type=MESH)

    loads = [
        pltpu.make_async_copy(src, dst, load_sem.at[i])
        for i, (src, dst) in enumerate([(stream_h, stream), (gain_h, gain), (wq_h, wq), (wkv_h, wkv), (k_h, kc), (v_h, vc), (lengths_h, lengths)])
    ]
    for c in loads[:4]:
        c.start()

    def wload(t):
        cols = pl.ds(pl.multiple_of(t * W, 128), W)
        return (
            pltpu.make_async_copy(wg_h.at[:, cols], wg.at[t], wsem.at[t, 0]),
            pltpu.make_async_copy(wu_h.at[:, cols], wu.at[t], wsem.at[t, 1]),
        )

    @pl.loop(0, T)
    def _(t):
        for c in wload(t):
            c.start()

    for c in loads[4:]:
        c.start()

    loads[0].wait()
    loads[1].wait()
    total = jnp.zeros((2, K), F32)
    for q in range(16):
        total += f32(stream[:, q * K:(q + 1) * K])
    mean = jnp.sum(total, axis=1, keepdims=True) * (1.0 / D)
    total = jnp.zeros((2, K), F32)
    for q in range(16):
        v = f32(stream[:, q * K:(q + 1) * K]) - mean
        total += v * v
    root = jnp.sqrt(jnp.sum(total, axis=1, keepdims=True) * (1.0 / D) + 1e-05)
    for q in range(16):
        v = (f32(stream[:, q * K:(q + 1) * K]) - mean) / root * gain[:, q * K:(q + 1) * K]
        nsend[q // 4, :, (q % 4) * K:(q % 4 + 1) * K] = v.astype(BF16)

    i = lax.broadcasted_iota(jnp.int32, (256, 256), 0)
    j = lax.broadcasted_iota(jnp.int32, (256, 256), 1)
    want = ((i >> 1) & 7) * 32 + ((i >> 4) & 3) * 8 + (i >> 6) * 2 + (i & 1)
    perm[...] = jnp.where(want == j, 1.0, 0.0).astype(BF16)
    vp[...] = jnp.zeros_like(vp)

    pl.semaphore_wait(bar, 13)

    first = [
        pltpu.make_async_remote_copy(
            nsend.at[h.at("y", k)], ybuf.at[h.y], d_ss.at[k], d_rs.at[k],
            device_id=h.dev("y", k), device_id_type=MESH)
        for k in (2, 1, 3)
    ]
    for c in first:
        c.start()
    ybuf[h.y] = nsend[h.y]
    for c in first:
        c.wait_recv()

    def zcols(zd):
        return pl.ds(pl.multiple_of(zd * K, 128), K)

    second = [
        pltpu.make_async_remote_copy(
            ybuf.at[:, :, zcols(h.at("z", k))], zbuf.at[h.z], d_ss.at[3 + k], d_rs.at[3 + k],
            device_id=h.dev("z", k), device_id_type=MESH)
        for k in (2, 1, 3)
    ]
    for c in second:
        c.start()

    def along(k):
        return lax.rem(h.gy + 2 * k, 8)

    def remote(src, dst, ss, rs, gy):
        return pltpu.make_async_remote_copy(
            src, dst, ss, rs, device_id=(h.gx, gy), device_id_type=MESH)

    def to_x(n, k):
        z = h.at("z", n)
        return remote(xr.at[h.gy, z], xr.at[h.gy, z], x_ss.at[n, k - 1], x_rs.at[n, k - 1], along(k))

    def to_other(k):
        z = h.at("z", 2)
        return remote(xr.at[h.gy, z], xr.at[h.gy, z], p_ss.at[2, k], p_rs.at[2, k], along(k) + 1 - 2 * h.c)

    def to_partner(n, k):
        if n == 2 and k:
            return to_other(k)
        g, z = along(4 - k), h.at("z", n)
        return remote(xr.at[g, z], xr.at[g, z], p_ss.at[n, k], p_rs.at[n, k], h.x * 2 + 1 - h.c)

    for n in (0, 1, 3, 2):
        z = h.at("z", n)
        if n == 0:
            for y in range(4):
                a8[n, 2 * y:2 * y + 2, :] = f32(ybuf[y, :, zcols(h.z)])
        else:
            second[{2: 0, 1: 1, 3: 2}[4 - n]].wait_recv()
            for y in range(4):
                a8[n, 2 * y:2 * y + 2, :] = f32(zbuf[z, y])
        xr[h.gy, z] = a8[n].astype(BF16)
        for k in (2, 1, 3):
            to_x(n, k).start()
            if n == 2:
                to_partner(n, k).start()
        to_partner(n, 0).start()
    for n in (0, 1, 3, 2):
        for k in (1, 3, 2):
            to_x(n, k).wait_recv()
            if n != 2:
                to_partner(n, k).start()
    for n in (0, 1, 3, 2):
        for k in range(4):
            to_partner(n, k).wait_recv()
    for n in range(3):
        cols = slice(n * 384, (n + 1) * 384)
        xs[:, cols] = jnp.dot(
            perm[...], xr[:, :, :, cols].reshape(256, 384), preferred_element_type=F32
        ).astype(BF16)
    att = [
        Stream(h, first, s, qp.at[n], qf1.at[n], qr1.at[n], qn1.at[n], qm.at[n], qf2.at[n], qr2.at[n], qn2.at[n],
               a_ss.at[n], a_rs.at[n])
        for n, (first, s) in enumerate([("y", -1), ("z", 1), ("y", 1)])
    ]
    att.append(Stream(h, "z", -1, vp, vf1, vr1, vn1, vm, vf2, vr2, vn2, a_ss.at[3], a_rs.at[3]))

    def ffn(t, n, order):
        return Stream(h, order, -1 if n == 0 else 1, fp.at[t, n], ff1.at[t, n], fr1.at[t, n], fn1.at[t, n],
                      fm.at[t, n], ff2.at[t, n], fr2.at[t, n], fn2.at[t, n], f_ss.at[t, n], f_rs.at[t, n])

    def pair(i, do):
        for t, order in ((2 * i, "y"), (2 * i + 1, "z")):
            do(t, [ffn(t, n, order) for n in (0, 1)])

    loads[2].wait()
    loads[3].wait()
    query = jnp.dot(xs[...], wq[...], preferred_element_type=F32)
    for n in range(3):
        qp[n] = query[:, n * DH:(n + 1) * DH].reshape(4, 4, 16, DH)
    vp[:, :, :, 0:64] = lax.dot_general(
        xs[...], wkv[...], (((1,), (1,)), ((), ())), preferred_element_type=F32
    ).reshape(4, 4, 16, 64)
    for s in att:
        s.start(0)

    def computes(lo, hi):
        @pl.loop(lo, hi)
        def _(i):
            pair(i, lambda t, ss: [c.wait() for c in wload(t)])
            for t in (2 * i, 2 * i + 1):
                for n, w in ((0, wg), (1, wu)):
                    fp[t, n] = jnp.dot(xs[...], w[t], preferred_element_type=F32).astype(BF16).reshape(4, 4, 16, W)
            pair(i, lambda t, ss: [s.start(0) for s in ss])

    def each(lo, hi, do):
        @pl.loop(lo, hi)
        def _(i):
            pair(i, lambda t, ss: [do(s) for s in ss])

    computes(0, 3)
    for s in att:
        s.relay(0)
    computes(3, T // 2)
    each(0, 3, lambda s: s.relay(0))
    for s in att:
        s.turn(True)
    each(3, T // 2, lambda s: s.relay(0))
    each(0, DIRECT, lambda s: s.turn())
    each(DIRECT, T // 2, lambda s: s.turn(True))

    for n, s in enumerate(att):
        val = s.total(1, True)
        for g in range(8):
            qs[g, :, n * DH:n * DH + val.shape[1]] = val[2 * g:2 * g + 2, :].astype(BF16)
    give = [
        pltpu.make_async_remote_copy(
            qs.at[lax.rem(h.gy + k, 8)], qr.at[h.gy], g_ss.at[k], g_rs.at[k],
            device_id=(h.gx, lax.rem(h.gy + k, 8)), device_id_type=MESH)
        for k in range(1, 8)
    ]
    for c in give:
        c.start()
    qr[h.gy] = qs[h.gy]
    each(0, DIRECT, lambda s: s.relay(1))

    for c in give:
        c.wait_recv()
    for g in range(8):
        for n in range(3):
            row = f32(qr[g, :, n * DH:(n + 1) * DH])
            for r in range(2):
                qa[r, g * 3 + n:g * 3 + n + 1, :] = row[r:r + 1, :]
        kvs[2 * g:2 * g + 2, :] = f32(qr[g, :, 768:896])
    moved = pltpu.roll(kvs[...], 64, axis=1)

    def whole(r, first):
        row = [(kvs[2 * g + r:2 * g + r + 1, :], moved[2 * g + r:2 * g + r + 1, :]) for g in range(first, first + 4)]
        return jnp.concatenate([row[0][0] + row[1][1], row[2][0] + row[3][1]], axis=1)

    for c in loads[4:]:
        c.wait()
    scale = DH ** (-0.5)
    for r in range(2):
        query = qa[r]
        scores = lax.dot_general(
            query.astype(BF16), kc[r], (((1,), (1,)), ((), ())), preferred_element_type=F32) * scale
        score_new = jnp.sum(query * whole(r, 0), axis=1, keepdims=True) * scale
        mask = lax.broadcasted_iota(jnp.int32, (HEADS, CACHE), 1) < lengths[r]
        top = jnp.maximum(jnp.max(jnp.where(mask, scores, -1e30), axis=1, keepdims=True), score_new)
        exponent = jnp.where(mask, jnp.exp(scores - top), 0.0)
        exponent_new = jnp.exp(score_new - top)
        total = jnp.sum(exponent, axis=1, keepdims=True) + exponent_new
        weights = (exponent / total).astype(BF16)
        weights_new = f32((exponent_new / total).astype(BF16))
        out = jnp.dot(weights, vc[r], preferred_element_type=F32) + weights_new * whole(r, 4)
        for n in range(HEADS):
            context[r:r + 1, n * DH:(n + 1) * DH] = out[n:n + 1, :].astype(BF16)

    def finish(direct, t, ss):
        gate, up = ss[0].total(1, direct), ss[1].total(1, direct)
        cols = pl.ds(pl.multiple_of(t * W, 128), W)
        hidden[:, cols] = (gate / (1.0 + jnp.exp(-gate)) * up).astype(BF16)

    @pl.loop(0, DIRECT)
    def _(i):
        pair(i, functools.partial(finish, False))

    @pl.loop(DIRECT, T // 2)
    def _(i):
        pair(i, functools.partial(finish, True))

    for c in first + second:
        c.wait_send()
    for n in range(4):
        for k in (1, 2, 3):
            to_x(n, k).wait_send()
        for k in range(4):
            to_partner(n, k).wait_send()
    for c in give:
        c.wait_send()
    for s in att:
        s.drain()

    each(0, T // 2, lambda s: s.drain())


def fused(stream, gain, w_gate, w_up, w_query, w_keyval, k_cache, v_cache, lengths):
    vm, dma = pltpu.VMEM, pltpu.SemaphoreType.DMA

    def rs(lead, wide, kind):
        return [
            vm(lead + (4, 4, 16, wide), kind),
            *[vm(lead + (4, 16, wide), kind)] * 3,
            vm(lead + (4, 16, wide), kind),
            *[vm(lead + (16, wide), kind)] * 3,
        ]

    return pl.pallas_call(
        kernel,
        out_shape=(
            vm((16, FF), BF16),
            vm((2, HEADS * DH), BF16),
        ),
        in_specs=[pl.BlockSpec(memory_space=pl.ANY)] * 9,
        out_specs=[pl.BlockSpec(memory_space=pltpu.VMEM)] * 2,
        scratch_shapes=[
            vm((2, D), BF16), vm((1, D), F32), vm((T, K, W), BF16), vm((T, K, W), BF16),
            vm((K, 768), BF16), vm((64, K), BF16), vm((2, CACHE, DH), BF16), vm((2, CACHE, DH), BF16),
            pltpu.SMEM((2,), jnp.int32), dma((7,)), dma((T, 2)),
            vm((4, 2, 4 * K), BF16), vm((4, 2, 4 * K), BF16), vm((4, 4, 2, K), BF16), vm((4, 8, K), F32),
            vm((8, 4, 8, K), BF16), vm((256, 256), BF16), vm((256, K), BF16),
            dma((7,)), dma((7,)), dma((4, 3)), dma((4, 3)), dma((4, 4)), dma((4, 4)),
            *rs((T, 2), W, BF16), dma((T, 2, 6)), dma((T, 2, 6)),
            *rs((3,), DH, F32),
            *rs((), 128, F32), dma((4, 6)), dma((4, 6)),
            vm((8, 2, 896), BF16), vm((8, 2, 896), BF16), vm((2, HEADS, DH), F32), vm((16, 128), F32),
            dma((8,)), dma((8,)),
        ],
        compiler_params=pltpu.CompilerParams(
            collective_id=0, has_side_effects=True, vmem_limit_bytes=62 * 2**20
        ),
    )(stream, gain, w_gate, w_up, w_query, w_keyval, k_cache, v_cache, lengths)


def body(stream, norm_gain, w_gate, w_up, w_query, w_keyval, k_cache, v_cache, lengths):
    hidden, context = fused(
        stream, norm_gain.reshape(1, D), w_gate, w_up, w_query, w_keyval.T, k_cache, v_cache, lengths
    )
    return (hidden, context)


def solution(mesh):
    return jax.shard_map(
        body,
        mesh=mesh,
        in_specs=(
            P(("gx", "gy"), None),
            P(),
            P("gx", "gy"),
            P("gx", "gy"),
            P("gx", "gy"),
            P("gx", "gy"),
            P(("gx", "gy"), None, None),
            P(("gx", "gy"), None, None),
            P(("gx", "gy")),
        ),
        out_specs=(P("gx", "gy"), P(("gx", "gy"), None)),
        check_vma=False,
    )
```

```python
import functools

import jax
import jax.numpy as jnp
from jax import lax
from jax.experimental import pallas as pl
from jax.experimental.pallas import tpu as pltpu
from jax.sharding import PartitionSpec as P

HEADS = 24
DH = 256
D = 18432
K = 1152
FF = 4608
T = 12
DIRECT = 4
CACHE = 512
W = FF // T
MESH = pl.DeviceIdType.MESH
F32 = jnp.float32
BF16 = jnp.bfloat16


def f32(v):
    return v.astype(F32)


class Place:
    def __init__(self):
        gx, self.gy = lax.axis_index("gx"), lax.axis_index("gy")
        self.y, self.z = lax.div(gx, 4), lax.rem(gx, 4)
        self.x, self.c = lax.div(self.gy, 2), lax.rem(self.gy, 2)
        self.gx = gx

    def at(self, axis, k):
        return lax.rem((self.y if axis == "y" else self.z) + (k % 4), 4)

    def dev(self, axis, k):
        if axis == "y":
            return (self.at("y", k) * 4 + self.z, self.gy)
        return (self.y * 4 + self.at("z", k), self.gy)


class Stream:
    def __init__(self, here, first, s, p, mid, far, rel, near, tmp, ss, rs):
        self.here, self.s, self.ss, self.rs = here, s, ss, rs
        second = "z" if first == "y" else "y"
        self.ax = (first, first, second)
        self.p, self.mid, self.tmp = p, mid, tmp
        self.far, self.rel, self.near = far, rel, near

    def own(self, ph, k):
        return (*self.p, self.mid)[ph].at[self.here.at(self.ax[ph], k)]

    def copy(self, ph, i, direct=False):
        s = self.s
        src, dst, k = (
            (self.own(ph, 2), self.far[ph], 2 if direct else s),
            (self.own(ph, -s), self.near[ph], -s),
            (self.own(ph, s) if direct else self.far[ph], self.rel[ph], s),
        )[i]
        return pltpu.make_async_remote_copy(
            src, dst, self.ss.at[ph * 3 + i], self.rs.at[ph * 2 + (i > 0)],
            device_id=self.here.dev(self.ax[ph], k), device_id_type=MESH,
        )

    def start(self, ph, direct=False):
        self.copy(ph, 0, direct).start()
        self.copy(ph, 1).start()
        if direct:
            self.copy(ph, 2, direct).start()

    def relay(self, ph):
        ref = self.far[ph]
        ref[...] = (f32(ref[...]) + f32(self.own(ph, self.s)[...])).astype(ref.dtype)
        self.copy(ph, 2).start()

    def total(self, ph, direct=False):
        value = f32(self.own(ph, 0)[...])
        if direct:
            value += f32(self.far[ph][...])
        return value + f32(self.rel[ph][...]) + f32(self.near[ph][...])

    def turn(self, direct=False):
        small, large = self.total(0), self.total(1)
        cols = slice(0, small.shape[1])
        for i in range(4):
            self.tmp[i, 0:4, cols] = small[4 * i:4 * i + 4]
            self.tmp[i, 4:16, cols] = large[12 * i:12 * i + 12]
        self.mid[...] = self.tmp[:, :, cols].astype(self.mid.dtype)
        self.start(2, direct)


def kernel(
    stream_h, gain_h, wg_h, wu_h, wq_h, wkv_h, k_h, v_h, lengths_h,
    hidden, context,
    stream, gain, wgu, wq, wkv, kc, vc, lengths, load_sem, wsem,
    nsend, ybuf, zbuf, a8, xr, perm0, perm1, xs0, xs1, tmp,
    d_ss, d_rs,
    *rest,
):
    fb, qb, vb = rest[0:9], rest[9:18], rest[18:27]
    f_ss, f_rs, q_ss, q_rs, v_ss, v_rs, qs, qr, qa, kvs, g_ss, g_rs = rest[27:]
    perm, xs = (perm0, perm1), (xs0, xs1)
    h = Place()
    bar = pltpu.get_barrier_semaphore()
    for ax in "yz":
        for k in (1, 2, 3):
            pl.semaphore_signal(bar, inc=1, device_id=h.dev(ax, k), device_id_type=MESH)
    for k in range(1, 8):
        pl.semaphore_signal(bar, inc=1, device_id=(h.gx, lax.rem(h.gy + k, 8)), device_id_type=MESH)

    loads = [
        pltpu.make_async_copy(src, dst, load_sem.at[i])
        for i, (src, dst) in enumerate([(stream_h, stream), (gain_h, gain), (wq_h, wq), (wkv_h, wkv), (k_h, kc), (v_h, vc), (lengths_h, lengths)])
    ]
    for c in loads[:4]:
        c.start()

    def wload(t):
        cols = pl.ds(pl.multiple_of(t * W, 128), W)
        return (
            pltpu.make_async_copy(wg_h.at[:, cols], wgu.at[t, 0], wsem.at[t // 2]),
            pltpu.make_async_copy(wu_h.at[:, cols], wgu.at[t, 1], wsem.at[t // 2]),
        )

    @pl.loop(0, T)
    def _(t):
        for c in wload(t):
            c.start()

    for c in loads[4:]:
        c.start()

    loads[0].wait()
    loads[1].wait()
    total = jnp.zeros((2, K), F32)
    for q in range(16):
        total += f32(stream[:, q * K:(q + 1) * K])
    mean = jnp.sum(total, axis=1, keepdims=True) * (1.0 / D)
    total = jnp.zeros((2, K), F32)
    for q in range(16):
        v = f32(stream[:, q * K:(q + 1) * K]) - mean
        total += v * v
    root = jnp.sqrt(jnp.sum(total, axis=1, keepdims=True) * (1.0 / D) + 1e-05)
    for q in range(16):
        v = (f32(stream[:, q * K:(q + 1) * K]) - mean) / root * gain[:, q * K:(q + 1) * K]
        nsend[q // 4, :, (q % 4) * K:(q % 4 + 1) * K] = v.astype(BF16)

    for part, m in ((0, 4), (1, 12)):
        i = lax.broadcasted_iota(jnp.int32, (16 * m, 16 * m), 0)
        j = lax.broadcasted_iota(jnp.int32, (16 * m, 16 * m), 1)
        y, z = (j >> 1) & 3, (j >> 3) & 3
        rest_of = (j >> 6) * 4 + ((j >> 5) & 1) * 2 + (j & 1)
        for order, (u, v) in enumerate(((y, z), (z, y))):
            perm[part][order] = jnp.where(i == u * (4 * m) + v * m + rest_of, 1.0, 0.0).astype(BF16)
    vb[0][...] = jnp.zeros_like(vb[0])
    vb[1][...] = jnp.zeros_like(vb[1])

    pl.semaphore_wait(bar, 13)

    def take(ref, sem):
        pltpu.make_async_remote_copy(
            ref, ref, sem, sem, device_id=h.dev("y", 1), device_id_type=MESH).wait_recv()

    def sent(ref, sem):
        pltpu.make_async_remote_copy(
            ref, ref, sem, sem, device_id=h.dev("y", 1), device_id_type=MESH).wait_send()

    first = [
        pltpu.make_async_remote_copy(
            nsend.at[h.at("y", k)], ybuf.at[h.y], d_ss.at[0], d_rs.at[0],
            device_id=h.dev("y", k), device_id_type=MESH)
        for k in (2, 1, 3)
    ]
    for c in first:
        c.start()
    ybuf[h.y] = nsend[h.y]
    take(ybuf.at[0:3], d_rs.at[0])

    def zcols(zd):
        return pl.ds(pl.multiple_of(zd * K, 128), K)

    second = [
        pltpu.make_async_remote_copy(
            ybuf.at[:, :, zcols(h.at("z", k))], zbuf.at[h.z], d_ss.at[1], d_rs.at[k],
            device_id=h.dev("z", k), device_id_type=MESH)
        for k in (2, 1, 3)
    ]
    for c in second:
        c.start()

    def along(k, flip):
        return lax.rem(h.x + k, 4) * 2 + lax.rem(h.c + flip, 2)

    def to_x(n, k, flip):
        z, slot = h.at("z", n), (4 - k) % 4
        return pltpu.make_async_remote_copy(
            xr.at[h.c, z], xr.at[slot * 2 + h.c, z], d_ss.at[2], d_rs.at[4 if k == 0 else 5],
            device_id=(h.gx, along(k, flip)), device_id_type=MESH)

    for n in (0, 1, 3, 2):
        z = h.at("z", n)
        if n == 0:
            for y in range(4):
                a8[n, 2 * y:2 * y + 2, :] = f32(ybuf[y, :, zcols(h.z)])
        else:
            second[{2: 0, 1: 1, 3: 2}[4 - n]].wait_recv()
            for y in range(4):
                a8[n, 2 * y:2 * y + 2, :] = f32(zbuf[z, y])
        xr[h.c, z] = a8[n].astype(BF16)
        for k, flip in ((0, 1), (3, 0), (3, 1), (2, 0), (2, 1), (1, 0), (1, 1)):
            to_x(n, k, flip).start()

    def rows(part):
        take(xr.at[0:(1, 6)[part]], d_rs.at[4 + part])
        for n in range(3):
            cols = slice(n * 384, (n + 1) * 384)
            got = xr[0:2, :, :, cols].reshape(64, 384) if part == 0 else xr[2:8, :, :, cols].reshape(192, 384)
            for order in (0, 1):
                xs[part][order, :, cols] = jnp.dot(
                    perm[part][order], got, preferred_element_type=F32).astype(BF16)

    def stream_of(b, lead, n, first, s, ss, rs):
        at = lead + (n,)
        return Stream(
            h, first, s, [b[0].at[at], b[1].at[at]], b[2].at[at], [r.at[at] for r in b[3:6]],
            [r.at[lead + (0, n)] for r in b[6:9]], [r.at[lead + (1, n)] for r in b[6:9]], tmp, ss, rs)

    att = [
        stream_of(qb, (), n, first, s, q_ss, q_rs)
        for n, (first, s) in enumerate([("y", -1), ("y", 1), ("z", 1)])
    ]
    att.append(stream_of(vb, (), 0, "z", -1, v_ss, v_rs))

    def att_take(ph, role):
        for b, sem in ((qb, q_rs), (vb, v_rs)):
            take(b[3 + 3 * role + ph], sem.at[ph * 2 + role])

    def pair_take(i, ph, role):
        take(fb[3 + 3 * role + ph].at[pl.ds(2 * i, 2)], f_rs.at[i, ph * 2 + role])

    def pair(i, do):
        for t, order in ((2 * i, "y"), (2 * i + 1, "z")):
            do(t, [stream_of(fb, (t,), n, order, -1 if n == 0 else 1, f_ss, f_rs.at[i]) for n in (0, 1)])

    def query(part):
        m = (16, 48)[part]
        val = jnp.dot(xs[part][0], wq[:, :2 * DH], preferred_element_type=F32)
        for n in range(2):
            qb[part][n] = val[:, n * DH:(n + 1) * DH].reshape(4, m, DH)
        qb[part][2] = jnp.dot(xs[part][1], wq[:, 2 * DH:], preferred_element_type=F32).reshape(4, m, DH)
        vb[part][0, :, :, 0:64] = lax.dot_general(
            xs[part][1], wkv[...], (((1,), (1,)), ((), ())), preferred_element_type=F32
        ).reshape(4, m, 64)
        for s in att:
            s.start(part)

    def computes(part, lo, hi):
        @pl.loop(lo, hi)
        def _(i):
            if part == 0:
                both = wgu.at[pl.ds(2 * i, 2)]
                pltpu.make_async_copy(both, both, wsem.at[i]).wait()
            for order in (0, 1):
                t = 2 * i + order
                for n in (0, 1):
                    val = jnp.dot(xs[part][order], wgu[t, n], preferred_element_type=F32)
                    fb[part][t, n] = val.astype(BF16).reshape(4, (16, 48)[part], W)
            pair(i, lambda t, ss: [s.start(part) for s in ss])

    def relays(ph, lo, hi):
        @pl.loop(lo, hi)
        def _(i):
            pair_take(i, ph, 0)
            pair(i, lambda t, ss: [s.relay(ph) for s in ss])

    def turns(lo, hi, direct):
        @pl.loop(lo, hi)
        def _(i):
            for ph in (0, 1):
                pair_take(i, ph, 1)
            pair(i, lambda t, ss: [s.turn(direct) for s in ss])

    def att_relay(ph):
        att_take(ph, 0)
        for s in att:
            s.relay(ph)

    rows(0)
    loads[2].wait()
    loads[3].wait()
    query(0)
    computes(0, 0, 4)
    att_relay(0)
    relays(0, 0, 2)
    computes(0, 4, T // 2)
    rows(1)
    query(1)
    computes(1, 0, 2)
    relays(0, 2, T // 2)
    computes(1, 2, 4)
    att_relay(1)
    computes(1, 4, T // 2)
    relays(1, 0, 3)
    for ph in (0, 1):
        att_take(ph, 1)
    for s in att:
        s.turn(True)
    relays(1, 3, T // 2)
    turns(0, DIRECT, False)
    turns(DIRECT, T // 2, True)

    att_take(2, 0)
    att_take(2, 1)
    for n, s in enumerate(att):
        val = s.total(2, True)
        for g in range(8):
            qs[g, :, n * DH:n * DH + val.shape[1]] = val[2 * g:2 * g + 2, :].astype(BF16)
    give = [
        pltpu.make_async_remote_copy(
            qs.at[2 * k + lax.rem(h.c + flip, 2)], qr.at[h.gy], g_ss.at[0], g_rs.at[0],
            device_id=(h.gx, along(k, flip)), device_id_type=MESH)
        for k in range(4) for flip in (0, 1) if k or flip
    ]
    for c in give:
        c.start()
    qr[h.gy] = qs[h.c]
    relays(2, 0, DIRECT)

    take(qr.at[0:7], g_rs.at[0])
    for g in range(8):
        for n in range(3):
            row = f32(qr[g, :, n * DH:(n + 1) * DH])
            for r in range(2):
                qa[r, g * 3 + n:g * 3 + n + 1, :] = row[r:r + 1, :]
        kvs[2 * g:2 * g + 2, :] = f32(qr[g, :, 768:896])
    moved = pltpu.roll(kvs[...], 64, axis=1)

    def whole(r, first):
        row = [(kvs[2 * g + r:2 * g + r + 1, :], moved[2 * g + r:2 * g + r + 1, :]) for g in range(first, first + 4)]
        return jnp.concatenate([row[0][0] + row[1][1], row[2][0] + row[3][1]], axis=1)

    for c in loads[4:]:
        c.wait()
    scale = DH ** (-0.5)
    for r in range(2):
        query = qa[r]
        scores = lax.dot_general(
            query.astype(BF16), kc[r], (((1,), (1,)), ((), ())), preferred_element_type=F32) * scale
        score_new = jnp.sum(query * whole(r, 0), axis=1, keepdims=True) * scale
        mask = lax.broadcasted_iota(jnp.int32, (HEADS, CACHE), 1) < lengths[r]
        top = jnp.maximum(jnp.max(jnp.where(mask, scores, -1e30), axis=1, keepdims=True), score_new)
        exponent = jnp.where(mask, jnp.exp(scores - top), 0.0)
        exponent_new = jnp.exp(score_new - top)
        total = jnp.sum(exponent, axis=1, keepdims=True) + exponent_new
        weights = (exponent / total).astype(BF16)
        weights_new = f32((exponent_new / total).astype(BF16))
        out = jnp.dot(weights, vc[r], preferred_element_type=F32) + weights_new * whole(r, 4)
        for n in range(HEADS):
            context[r:r + 1, n * DH:(n + 1) * DH] = out[n:n + 1, :].astype(BF16)

    def finish(direct, t, ss):
        gate, up = (s.total(2, direct) for s in ss)
        cols = pl.ds(pl.multiple_of(t * W, 128), W)
        val = gate / (1.0 + jnp.exp(-gate)) * up
        val = jnp.where(h.x % 2 == 1, jnp.roll(val, 4, axis=0), val)
        val = jnp.where(h.x >= 2, jnp.roll(val, 8, axis=0), val)
        hidden[:, cols] = val.astype(BF16)

    @pl.loop(0, DIRECT)
    def _(i):
        pair_take(i, 2, 1)
        pair(i, functools.partial(finish, False))

    @pl.loop(DIRECT, T // 2)
    def _(i):
        pair_take(i, 2, 0)
        pair_take(i, 2, 1)
        pair(i, functools.partial(finish, True))

    sent(ybuf.at[0:3], d_ss.at[0])
    sent(zbuf.at[0:3], d_ss.at[1])
    sent(xr.at[0:7], d_ss.at[2])
    sent(qr.at[0:7], g_ss.at[0])
    for b, ss in ((fb, f_ss), (qb, q_ss), (vb, v_ss)):
        for ph in range(3):
            for i in range(3):
                sent(b[3 + ph], ss.at[ph * 3 + i])


def fused(stream, gain, w_gate, w_up, w_query, w_keyval, k_cache, v_cache, lengths):
    vm, dma = pltpu.VMEM, pltpu.SemaphoreType.DMA

    def rs(lead, wide, kind):
        ms = (16, 48, 16)
        return [
            *[vm(lead + (4, m, wide), kind) for m in ms],
            *[vm(lead + (m, wide), kind) for m in ms],
            *[vm(lead[:-1] + (2,) + lead[-1:] + (m, wide), kind) for m in ms],
        ]

    return pl.pallas_call(
        kernel,
        out_shape=(
            vm((16, FF), BF16),
            vm((2, HEADS * DH), BF16),
        ),
        in_specs=[pl.BlockSpec(memory_space=pl.ANY)] * 9,
        out_specs=[pl.BlockSpec(memory_space=pltpu.VMEM)] * 2,
        scratch_shapes=[
            vm((2, D), BF16), vm((1, D), F32), vm((T, 2, K, W), BF16),
            vm((K, 768), BF16), vm((64, K), BF16), vm((2, CACHE, DH), BF16), vm((2, CACHE, DH), BF16),
            pltpu.SMEM((2,), jnp.int32), dma((7,)), dma((T // 2,)),
            vm((4, 2, 4 * K), BF16), vm((4, 2, 4 * K), BF16), vm((4, 4, 2, K), BF16), vm((4, 8, K), F32),
            vm((8, 4, 8, K), BF16), vm((2, 64, 64), BF16), vm((2, 192, 192), BF16),
            vm((2, 64, K), BF16), vm((2, 192, K), BF16), vm((4, 16, W), F32),
            dma((3,)), dma((6,)),
            *rs((T, 2), W, BF16), *rs((3,), DH, F32), *rs((1,), 128, F32),
            dma((9,)), dma((T // 2, 6)), dma((9,)), dma((6,)), dma((9,)), dma((6,)),
            vm((8, 2, 896), BF16), vm((8, 2, 896), BF16), vm((2, HEADS, DH), F32), vm((16, 128), F32),
            dma((1,)), dma((1,)),
        ],
        compiler_params=pltpu.CompilerParams(
            collective_id=0, has_side_effects=True, vmem_limit_bytes=62 * 2**20
        ),
    )(stream, gain, w_gate, w_up, w_query, w_keyval, k_cache, v_cache, lengths)


def body(stream, norm_gain, w_gate, w_up, w_query, w_keyval, k_cache, v_cache, lengths):
    hidden, context = fused(
        stream, norm_gain.reshape(1, D), w_gate, w_up, w_query, w_keyval.T, k_cache, v_cache, lengths
    )
    return (hidden, context)


def solution(mesh):
    return jax.shard_map(
        body,
        mesh=mesh,
        in_specs=(
            P(("gx", "gy"), None),
            P(),
            P("gx", "gy"),
            P("gx", "gy"),
            P("gx", "gy"),
            P("gx", "gy"),
            P(("gx", "gy"), None, None),
            P(("gx", "gy"), None, None),
            P(("gx", "gy")),
        ),
        out_specs=(P("gx", "gy"), P(("gx", "gy"), None)),
        check_vma=False,
    )
```

```python
import functools

import jax
import jax.numpy as jnp
from jax import lax
from jax.experimental import pallas as pl
from jax.experimental.pallas import tpu as pltpu
from jax.sharding import PartitionSpec as P

HEADS = 24
DH = 256
D = 18432
K = 1152
FF = 4608
T = 12
DIRECT = 4
CACHE = 512
W = FF // T
MESH = pl.DeviceIdType.MESH
F32 = jnp.float32
BF16 = jnp.bfloat16


def f32(v):
    return v.astype(F32)


class Place:
    def __init__(self):
        gx, self.gy = lax.axis_index("gx"), lax.axis_index("gy")
        self.y, self.z = lax.div(gx, 4), lax.rem(gx, 4)
        self.x, self.c = lax.div(self.gy, 2), lax.rem(self.gy, 2)
        self.gx = gx

    def at(self, axis, k):
        return lax.rem((self.y if axis == "y" else self.z) + (k % 4), 4)

    def dev(self, axis, k):
        if axis == "y":
            return (self.at("y", k) * 4 + self.z, self.gy)
        return (self.y * 4 + self.at("z", k), self.gy)


class Stream:
    def __init__(self, here, first, s, p, mid, far, rel, near, tmp, ss, rs):
        self.here, self.s, self.ss, self.rs = here, s, ss, rs
        second = "z" if first == "y" else "y"
        self.ax = (first, first, second)
        self.p, self.mid, self.tmp = p, mid, tmp
        self.far, self.rel, self.near = far, rel, near

    def own(self, ph, k):
        return (*self.p, self.mid)[ph].at[self.here.at(self.ax[ph], k)]

    def copy(self, ph, i, direct=False):
        s = self.s
        src, dst, k = (
            (self.own(ph, 2), self.far[ph], 2 if direct else s),
            (self.own(ph, -s), self.near[ph], -s),
            (self.own(ph, s) if direct else self.far[ph], self.rel[ph], s),
        )[i]
        return pltpu.make_async_remote_copy(
            src, dst, self.ss.at[ph * 3 + i], self.rs.at[ph * 2 + (i > 0)],
            device_id=self.here.dev(self.ax[ph], k), device_id_type=MESH,
        )

    def start(self, ph, direct=False):
        self.copy(ph, 0, direct).start()
        self.copy(ph, 1).start()
        if direct:
            self.copy(ph, 2, direct).start()

    def relay(self, ph):
        ref = self.far[ph]
        ref[...] = (f32(ref[...]) + f32(self.own(ph, self.s)[...])).astype(ref.dtype)
        self.copy(ph, 2).start()

    def total(self, ph, direct=False):
        value = f32(self.own(ph, 0)[...])
        if direct:
            value += f32(self.far[ph][...])
        return value + f32(self.rel[ph][...]) + f32(self.near[ph][...])

    def turn(self, direct=False):
        small, large = self.total(0), self.total(1)
        cols = slice(0, small.shape[1])
        for i in range(4):
            self.tmp[i, 0:4, cols] = small[4 * i:4 * i + 4]
            self.tmp[i, 4:16, cols] = large[12 * i:12 * i + 12]
        self.mid[...] = self.tmp[:, :, cols].astype(self.mid.dtype)
        self.start(2, direct)


def kernel(
    stream_h, gain_h, wg_h, wu_h, wq_h, wkv_h, k_h, v_h, lengths_h,
    hidden, context,
    stream, gain, wgu, wq, wkv, kc, vc, lengths, load_sem, wsem,
    nsend, ybuf, zbuf, a8, xr, perm0, perm1, xs0, xs1, tmp, both, join,
    d_ss, d_rs,
    *rest,
):
    fb, qb, vb = rest[0:9], rest[9:18], rest[18:27]
    f_ss, f_rs, q_ss, q_rs, v_ss, v_rs, qs, qr, qa, kvs, g_ss, g_rs = rest[27:]
    perm, xs = (perm0, perm1), (xs0, xs1)
    h = Place()
    loads = [
        pltpu.make_async_copy(src, dst, load_sem.at[i])
        for i, (src, dst) in enumerate([(stream_h, stream), (gain_h, gain), (wq_h, wq), (wkv_h, wkv), (k_h, kc), (v_h, vc), (lengths_h, lengths)])
    ]
    for c in loads[:2]:
        c.start()

    bar = pltpu.get_barrier_semaphore()
    for ax in "yz":
        for k in (1, 2, 3):
            pl.semaphore_signal(bar, inc=1, device_id=h.dev(ax, k), device_id_type=MESH)
    for k in range(1, 8):
        pl.semaphore_signal(bar, inc=1, device_id=(h.gx, lax.rem(h.gy + k, 8)), device_id_type=MESH)

    loads[0].wait()
    loads[1].wait()
    total = jnp.zeros((2, K), F32)
    for q in range(16):
        total += f32(stream[:, q * K:(q + 1) * K])
    mean = jnp.sum(total, axis=1, keepdims=True) * (1.0 / D)
    total = jnp.zeros((2, K), F32)
    for q in range(16):
        v = f32(stream[:, q * K:(q + 1) * K]) - mean
        total += v * v
    root = jnp.sqrt(jnp.sum(total, axis=1, keepdims=True) * (1.0 / D) + 1e-05)
    for q in range(16):
        v = (f32(stream[:, q * K:(q + 1) * K]) - mean) / root * gain[:, q * K:(q + 1) * K]
        nsend[q // 4, :, (q % 4) * K:(q % 4 + 1) * K] = v.astype(BF16)

    pl.semaphore_wait(bar, 13)

    def take(ref, sem):
        pltpu.make_async_remote_copy(
            ref, ref, sem, sem, device_id=h.dev("y", 1), device_id_type=MESH).wait_recv()

    def sent(ref, sem):
        pltpu.make_async_remote_copy(
            ref, ref, sem, sem, device_id=h.dev("y", 1), device_id_type=MESH).wait_send()

    first = [
        pltpu.make_async_remote_copy(
            nsend.at[h.at("y", k)], ybuf.at[h.y], d_ss.at[0], d_rs.at[0],
            device_id=h.dev("y", k), device_id_type=MESH)
        for k in (2, 1, 3)
    ]
    for c in first:
        c.start()
    ybuf[h.y] = nsend[h.y]
    for c in loads[2:4]:
        c.start()

    def wload(t):
        cols = pl.ds(pl.multiple_of(t * W, 128), W)
        return (
            pltpu.make_async_copy(wg_h.at[:, cols], wgu.at[t, 0], wsem.at[t // 2]),
            pltpu.make_async_copy(wu_h.at[:, cols], wgu.at[t, 1], wsem.at[t // 2]),
        )

    @pl.loop(0, T)
    def _(t):
        for c in wload(t):
            c.start()

    for c in loads[4:]:
        c.start()

    for part, m in ((0, 4), (1, 12)):
        i = lax.broadcasted_iota(jnp.int32, (16 * m, 16 * m), 0)
        j = lax.broadcasted_iota(jnp.int32, (16 * m, 16 * m), 1)
        y, z = (j >> 1) & 3, (j >> 3) & 3
        rest_of = (j >> 6) * 4 + ((j >> 5) & 1) * 2 + (j & 1)
        for order, (u, v) in enumerate(((y, z), (z, y))):
            perm[part][order] = jnp.where(i == u * (4 * m) + v * m + rest_of, 1.0, 0.0).astype(BF16)
    i = lax.broadcasted_iota(jnp.int32, (64, 64), 0)
    j = lax.broadcasted_iota(jnp.int32, (64, 64), 1)
    k, q = i >> 4, i & 15
    join[...] = jnp.where(j == jnp.where(q < 4, k * 4 + q, 12 + k * 12 + q), 1.0, 0.0).astype(BF16)
    vb[0][...] = jnp.zeros_like(vb[0])
    vb[1][...] = jnp.zeros_like(vb[1])

    take(ybuf.at[0:3], d_rs.at[0])

    def zcols(zd):
        return pl.ds(pl.multiple_of(zd * K, 128), K)

    second = [
        pltpu.make_async_remote_copy(
            ybuf.at[:, :, zcols(h.at("z", k))], zbuf.at[h.z], d_ss.at[1], d_rs.at[k],
            device_id=h.dev("z", k), device_id_type=MESH)
        for k in (2, 1, 3)
    ]
    for c in second:
        c.start()

    def along(k, flip):
        return lax.rem(h.x + k, 4) * 2 + lax.rem(h.c + flip, 2)

    def to_x(n, k, flip):
        z, slot = h.at("z", n), (4 - k) % 4
        return pltpu.make_async_remote_copy(
            xr.at[h.c, z], xr.at[slot * 2 + h.c, z], d_ss.at[2], d_rs.at[4 if k == 0 else 5],
            device_id=(h.gx, along(k, flip)), device_id_type=MESH)

    for n in (0, 1, 3, 2):
        z = h.at("z", n)
        if n == 0:
            for y in range(4):
                a8[n, 2 * y:2 * y + 2, :] = f32(ybuf[y, :, zcols(h.z)])
        else:
            second[{2: 0, 1: 1, 3: 2}[4 - n]].wait_recv()
            for y in range(4):
                a8[n, 2 * y:2 * y + 2, :] = f32(zbuf[z, y])
        xr[h.c, z] = a8[n].astype(BF16)
        for k, flip in ((0, 1), (3, 0), (3, 1), (2, 0), (2, 1), (1, 0), (1, 1)):
            to_x(n, k, flip).start()

    def rows(part):
        take(xr.at[0:(1, 6)[part]], d_rs.at[4 + part])
        for n in range(3):
            cols = slice(n * 384, (n + 1) * 384)
            got = xr[0:2, :, :, cols].reshape(64, 384) if part == 0 else xr[2:8, :, :, cols].reshape(192, 384)
            for order in (0, 1):
                xs[part][order, :, cols] = jnp.dot(
                    perm[part][order], got, preferred_element_type=F32).astype(BF16)

    def stream_of(b, lead, n, first, s, ss, rs):
        at = lead + (n,)
        return Stream(
            h, first, s, [b[0].at[at], b[1].at[at]], b[2].at[at], [r.at[at] for r in b[3:6]],
            [r.at[lead + (0, n)] for r in b[6:9]], [r.at[lead + (1, n)] for r in b[6:9]], tmp, ss, rs)

    att = [
        stream_of(qb, (), n, first, s, q_ss, q_rs)
        for n, (first, s) in enumerate([("y", -1), ("y", 1), ("z", 1)])
    ]
    att.append(stream_of(vb, (), 0, "z", -1, v_ss, v_rs))

    def att_take(ph, role):
        for b, sem in ((qb, q_rs), (vb, v_rs)):
            take(b[3 + 3 * role + ph], sem.at[ph * 2 + role])

    def pair_take(i, ph, role):
        take(fb[3 + 3 * role + ph].at[pl.ds(2 * i, 2)], f_rs.at[i, ph * 2 + role])

    def pair(i, do):
        for t, order in ((2 * i, "y"), (2 * i + 1, "z")):
            do(t, [stream_of(fb, (t,), n, order, -1 if n == 0 else 1, f_ss, f_rs.at[i]) for n in (0, 1)])

    def query(part):
        m = (16, 48)[part]
        val = jnp.dot(xs[part][0], wq[:, :2 * DH], preferred_element_type=F32)
        for n in range(2):
            qb[part][n] = val[:, n * DH:(n + 1) * DH].reshape(4, m, DH)
        qb[part][2] = jnp.dot(xs[part][1], wq[:, 2 * DH:], preferred_element_type=F32).reshape(4, m, DH)
        vb[part][0, :, :, 0:64] = lax.dot_general(
            xs[part][1], wkv[...], (((1,), (1,)), ((), ())), preferred_element_type=F32
        ).reshape(4, m, 64)
        for s in att:
            s.start(part)

    def computes(part, lo, hi):
        @pl.loop(lo, hi)
        def _(i):
            if part == 0:
                blocks = wgu.at[pl.ds(2 * i, 2)]
                pltpu.make_async_copy(blocks, blocks, wsem.at[i]).wait()
            for order in (0, 1):
                t = 2 * i + order
                for n in (0, 1):
                    val = jnp.dot(xs[part][order], wgu[t, n], preferred_element_type=F32)
                    fb[part][t, n] = val.astype(BF16).reshape(4, (16, 48)[part], W)
            pair(i, lambda t, ss: [s.start(part) for s in ss])

    def relays(ph, lo, hi):
        @pl.loop(lo, hi)
        def _(i):
            pair_take(i, ph, 0)
            pair(i, lambda t, ss: [s.relay(ph) for s in ss])

    def turns(lo, hi, direct):
        @pl.loop(lo, hi)
        def _(i):
            for ph in (0, 1):
                pair_take(i, ph, 1)
            group = []
            pair(i, lambda t, ss: group.extend(ss))
            for n, s in enumerate(group):
                cols = slice(n * W, (n + 1) * W)
                both[0:16, cols] = s.total(0).astype(BF16)
                both[16:64, cols] = s.total(1).astype(BF16)
            for n, s in enumerate(group):
                val = jnp.dot(join[...], both[:, n * W:(n + 1) * W], preferred_element_type=F32)
                s.mid[...] = val.astype(BF16).reshape(4, 16, W)
            for s in group:
                s.start(2, direct)

    def att_relay(ph):
        att_take(ph, 0)
        for s in att:
            s.relay(ph)

    rows(0)
    loads[2].wait()
    loads[3].wait()
    query(0)
    computes(0, 0, T // 2)
    rows(1)
    query(1)
    att_relay(0)
    relays(0, 0, 4)
    computes(1, 0, 2)
    relays(0, 4, T // 2)
    computes(1, 2, 4)
    att_relay(1)
    computes(1, 4, T // 2)
    relays(1, 0, 3)
    for ph in (0, 1):
        att_take(ph, 1)
    for s in att:
        s.turn(True)
    relays(1, 3, T // 2)
    turns(0, DIRECT, False)

    att_take(2, 0)
    att_take(2, 1)
    for n, s in enumerate(att):
        val = s.total(2, True)
        for g in range(8):
            qs[g, :, n * DH:n * DH + val.shape[1]] = val[2 * g:2 * g + 2, :].astype(BF16)
    give = [
        pltpu.make_async_remote_copy(
            qs.at[2 * k + lax.rem(h.c + flip, 2)], qr.at[h.gy], g_ss.at[0], g_rs.at[0],
            device_id=(h.gx, along(k, flip)), device_id_type=MESH)
        for k in range(4) for flip in (0, 1) if k or flip
    ]
    for c in give:
        c.start()
    qr[h.gy] = qs[h.c]
    turns(DIRECT, T // 2, True)

    relays(2, 0, DIRECT)

    take(qr.at[0:7], g_rs.at[0])
    for g in range(8):
        for n in range(3):
            row = f32(qr[g, :, n * DH:(n + 1) * DH])
            for r in range(2):
                qa[r, g * 3 + n:g * 3 + n + 1, :] = row[r:r + 1, :]
        kvs[2 * g:2 * g + 2, :] = f32(qr[g, :, 768:896])
    moved = pltpu.roll(kvs[...], 64, axis=1)

    def whole(r, first):
        row = [(kvs[2 * g + r:2 * g + r + 1, :], moved[2 * g + r:2 * g + r + 1, :]) for g in range(first, first + 4)]
        return jnp.concatenate([row[0][0] + row[1][1], row[2][0] + row[3][1]], axis=1)

    for c in loads[4:]:
        c.wait()
    scale = DH ** (-0.5)
    for r in range(2):
        query = qa[r]
        scores = lax.dot_general(
            query.astype(BF16), kc[r], (((1,), (1,)), ((), ())), preferred_element_type=F32) * scale
        score_new = jnp.sum(query * whole(r, 0), axis=1, keepdims=True) * scale
        mask = lax.broadcasted_iota(jnp.int32, (HEADS, CACHE), 1) < lengths[r]
        top = jnp.maximum(jnp.max(jnp.where(mask, scores, -1e30), axis=1, keepdims=True), score_new)
        exponent = jnp.where(mask, jnp.exp(scores - top), 0.0)
        exponent_new = jnp.exp(score_new - top)
        total = jnp.sum(exponent, axis=1, keepdims=True) + exponent_new
        weights = (exponent / total).astype(BF16)
        weights_new = f32((exponent_new / total).astype(BF16))
        out = jnp.dot(weights, vc[r], preferred_element_type=F32) + weights_new * whole(r, 4)
        for n in range(HEADS):
            context[r:r + 1, n * DH:(n + 1) * DH] = out[n:n + 1, :].astype(BF16)

    def finish(direct, t, ss):
        gate, up = (s.total(2, direct) for s in ss)
        cols = pl.ds(pl.multiple_of(t * W, 128), W)
        val = gate / (1.0 + jnp.exp(-gate)) * up
        val = jnp.where(h.x % 2 == 1, jnp.roll(val, 4, axis=0), val)
        val = jnp.where(h.x >= 2, jnp.roll(val, 8, axis=0), val)
        hidden[:, cols] = val.astype(BF16)

    @pl.loop(0, DIRECT)
    def _(i):
        pair_take(i, 2, 1)
        pair(i, functools.partial(finish, False))

    @pl.loop(DIRECT, T // 2)
    def _(i):
        pair_take(i, 2, 0)
        pair_take(i, 2, 1)
        pair(i, functools.partial(finish, True))

    sent(ybuf.at[0:3], d_ss.at[0])
    sent(zbuf.at[0:3], d_ss.at[1])
    sent(xr.at[0:7], d_ss.at[2])
    sent(qr.at[0:7], g_ss.at[0])
    for b, ss in ((fb, f_ss), (qb, q_ss), (vb, v_ss)):
        for ph in range(3):
            for i in range(3):
                sent(b[3 + ph], ss.at[ph * 3 + i])


def fused(stream, gain, w_gate, w_up, w_query, w_keyval, k_cache, v_cache, lengths):
    vm, dma = pltpu.VMEM, pltpu.SemaphoreType.DMA

    def rs(lead, wide, kind):
        ms = (16, 48, 16)
        return [
            *[vm(lead + (4, m, wide), kind) for m in ms],
            *[vm(lead + (m, wide), kind) for m in ms],
            *[vm(lead[:-1] + (2,) + lead[-1:] + (m, wide), kind) for m in ms],
        ]

    return pl.pallas_call(
        kernel,
        out_shape=(
            vm((16, FF), BF16),
            vm((2, HEADS * DH), BF16),
        ),
        in_specs=[pl.BlockSpec(memory_space=pl.ANY)] * 9,
        out_specs=[pl.BlockSpec(memory_space=pltpu.VMEM)] * 2,
        scratch_shapes=[
            vm((2, D), BF16), vm((1, D), F32), vm((T, 2, K, W), BF16),
            vm((K, 768), BF16), vm((64, K), BF16), vm((2, CACHE, DH), BF16), vm((2, CACHE, DH), BF16),
            pltpu.SMEM((2,), jnp.int32), dma((7,)), dma((T // 2,)),
            vm((4, 2, 4 * K), BF16), vm((4, 2, 4 * K), BF16), vm((4, 4, 2, K), BF16), vm((4, 8, K), F32),
            vm((8, 4, 8, K), BF16), vm((2, 64, 64), BF16), vm((2, 192, 192), BF16),
            vm((2, 64, K), BF16), vm((2, 192, K), BF16), vm((4, 16, W), F32),
            vm((64, 4 * W), BF16), vm((64, 64), BF16),
            dma((3,)), dma((6,)),
            *rs((T, 2), W, BF16), *rs((3,), DH, F32), *rs((1,), 128, F32),
            dma((9,)), dma((T // 2, 6)), dma((9,)), dma((6,)), dma((9,)), dma((6,)),
            vm((8, 2, 896), BF16), vm((8, 2, 896), BF16), vm((2, HEADS, DH), F32), vm((16, 128), F32),
            dma((1,)), dma((1,)),
        ],
        compiler_params=pltpu.CompilerParams(
            collective_id=0, has_side_effects=True, vmem_limit_bytes=62 * 2**20
        ),
    )(stream, gain, w_gate, w_up, w_query, w_keyval, k_cache, v_cache, lengths)


def write(hidden, context, hidden_h, context_h, sem):
    copies = [
        pltpu.make_async_copy(hidden, hidden_h, sem.at[0]),
        pltpu.make_async_copy(context, context_h, sem.at[1]),
    ]
    for c in copies:
        c.start()
    for c in copies:
        c.wait()


def body(stream, norm_gain, w_gate, w_up, w_query, w_keyval, k_cache, v_cache, lengths):
    hidden, context = fused(
        stream, norm_gain.reshape(1, D), w_gate, w_up, w_query, w_keyval.T, k_cache, v_cache, lengths
    )
    return pl.pallas_call(
        write,
        out_shape=(
            jax.ShapeDtypeStruct((16, FF), BF16),
            jax.ShapeDtypeStruct((2, HEADS * DH), BF16),
        ),
        in_specs=[pl.BlockSpec(memory_space=pl.ANY)] * 2,
        out_specs=[pl.BlockSpec(memory_space=pl.ANY)] * 2,
        scratch_shapes=[pltpu.SemaphoreType.DMA((2,))],
    )(*(pltpu.with_memory_space_constraint(v, pltpu.VMEM) for v in (hidden, context)))


def solution(mesh):
    return jax.shard_map(
        body,
        mesh=mesh,
        in_specs=(
            P(("gx", "gy"), None),
            P(),
            P("gx", "gy"),
            P("gx", "gy"),
            P("gx", "gy"),
            P("gx", "gy"),
            P(("gx", "gy"), None, None),
            P(("gx", "gy"), None, None),
            P(("gx", "gy")),
        ),
        out_specs=(P("gx", "gy"), P(("gx", "gy"), None)),
        check_vma=False,
    )
```

```python
import functools

import jax
import jax.numpy as jnp
from jax import lax
from jax.experimental import pallas as pl
from jax.experimental.pallas import tpu as pltpu
from jax.sharding import PartitionSpec as P

HEADS = 24
DH = 256
D = 18432
K = 1152
FF = 4608
T = 12
DIRECT = 4
CACHE = 512
W = FF // T
MESH = pl.DeviceIdType.MESH
F32 = jnp.float32
BF16 = jnp.bfloat16


def f32(v):
    return v.astype(F32)


class Place:
    def __init__(self):
        gx, self.gy = lax.axis_index("gx"), lax.axis_index("gy")
        self.y, self.z = lax.div(gx, 4), lax.rem(gx, 4)
        self.x, self.c = lax.div(self.gy, 2), lax.rem(self.gy, 2)
        self.gx = gx

    def at(self, axis, k):
        return lax.rem((self.y if axis == "y" else self.z) + (k % 4), 4)

    def dev(self, axis, k):
        if axis == "y":
            return (self.at("y", k) * 4 + self.z, self.gy)
        return (self.y * 4 + self.at("z", k), self.gy)


class Stream:
    def __init__(self, here, first, s, p, mid, far, rel, near, tmp, ss, rs):
        self.here, self.s, self.ss, self.rs = here, s, ss, rs
        second = "z" if first == "y" else "y"
        self.ax = (first, first, second)
        self.p, self.mid, self.tmp = p, mid, tmp
        self.far, self.rel, self.near = far, rel, near

    def own(self, ph, k):
        return (*self.p, self.mid)[ph].at[self.here.at(self.ax[ph], k)]

    def copy(self, ph, i, direct=False):
        s = self.s
        src, dst, k = (
            (self.own(ph, 2), self.far[ph], 2 if direct else s),
            (self.own(ph, -s), self.near[ph], -s),
            (self.own(ph, s) if direct else self.far[ph], self.rel[ph], s),
        )[i]
        return pltpu.make_async_remote_copy(
            src, dst, self.ss.at[ph * 3 + i], self.rs.at[ph * 2 + (i > 0)],
            device_id=self.here.dev(self.ax[ph], k), device_id_type=MESH,
        )

    def start(self, ph, direct=False):
        self.copy(ph, 0, direct).start()
        self.copy(ph, 1).start()
        if direct:
            self.copy(ph, 2, direct).start()

    def relay(self, ph):
        ref = self.far[ph]
        ref[...] = (f32(ref[...]) + f32(self.own(ph, self.s)[...])).astype(ref.dtype)
        self.copy(ph, 2).start()

    def total(self, ph, direct=False):
        value = f32(self.own(ph, 0)[...])
        if direct:
            value += f32(self.far[ph][...])
        return value + f32(self.rel[ph][...]) + f32(self.near[ph][...])

    def turn(self, direct=False):
        small, large = self.total(0), self.total(1)
        cols = slice(0, small.shape[1])
        for i in range(4):
            self.tmp[i, 0:4, cols] = small[4 * i:4 * i + 4]
            self.tmp[i, 4:16, cols] = large[12 * i:12 * i + 12]
        self.mid[...] = self.tmp[:, :, cols].astype(self.mid.dtype)
        self.start(2, direct)


def kernel(
    stream_h, gain_h, wg_h, wu_h, wq_h, wkv_h, k_h, v_h, lengths_h,
    hidden, context,
    stream, gain, wgu, wq, wkv, kc, vc, lengths, load_sem, wsem,
    nsend, ybuf, zbuf, a8, xr, perm0, perm1, xs0, xs1, tmp, both, join,
    d_ss, d_rs,
    *rest,
):
    fb, qb, vb = rest[0:9], rest[9:18], rest[18:27]
    f_ss, f_rs, q_ss, q_rs, v_ss, v_rs, qs, qr, qa, kvs, g_ss, g_rs = rest[27:]
    perm, xs = (perm0, perm1), (xs0, xs1)
    h = Place()
    loads = [
        pltpu.make_async_copy(src, dst, load_sem.at[i])
        for i, (src, dst) in enumerate([(stream_h, stream), (gain_h, gain), (wq_h, wq), (wkv_h, wkv), (k_h, kc), (v_h, vc), (lengths_h, lengths)])
    ]
    for c in loads[:2]:
        c.start()

    bar = pltpu.get_barrier_semaphore()
    for ax in "yz":
        for k in (1, 2, 3):
            pl.semaphore_signal(bar, inc=1, device_id=h.dev(ax, k), device_id_type=MESH)
    for k in range(1, 8):
        pl.semaphore_signal(bar, inc=1, device_id=(h.gx, lax.rem(h.gy + k, 8)), device_id_type=MESH)

    loads[0].wait()
    loads[1].wait()
    total = jnp.zeros((2, K), F32)
    for q in range(16):
        total += f32(stream[:, q * K:(q + 1) * K])
    mean = jnp.sum(total, axis=1, keepdims=True) * (1.0 / D)
    total = jnp.zeros((2, K), F32)
    for q in range(16):
        v = f32(stream[:, q * K:(q + 1) * K]) - mean
        total += v * v
    root = jnp.sqrt(jnp.sum(total, axis=1, keepdims=True) * (1.0 / D) + 1e-05)
    for q in range(16):
        v = (f32(stream[:, q * K:(q + 1) * K]) - mean) / root * gain[:, q * K:(q + 1) * K]
        nsend[q // 4, :, (q % 4) * K:(q % 4 + 1) * K] = v.astype(BF16)

    pl.semaphore_wait(bar, 13)

    def take(ref, sem):
        pltpu.make_async_remote_copy(
            ref, ref, sem, sem, device_id=h.dev("y", 1), device_id_type=MESH).wait_recv()

    def sent(ref, sem):
        pltpu.make_async_remote_copy(
            ref, ref, sem, sem, device_id=h.dev("y", 1), device_id_type=MESH).wait_send()

    first = [
        pltpu.make_async_remote_copy(
            nsend.at[h.at("y", k)], ybuf.at[h.y], d_ss.at[0], d_rs.at[0],
            device_id=h.dev("y", k), device_id_type=MESH)
        for k in (2, 1, 3)
    ]
    for c in first:
        c.start()
    ybuf[h.y] = nsend[h.y]
    for c in loads[2:4]:
        c.start()

    def wload(t):
        cols = pl.ds(pl.multiple_of(t * W, 128), W)
        return (
            pltpu.make_async_copy(wg_h.at[:, cols], wgu.at[t, 0], wsem.at[t // 2]),
            pltpu.make_async_copy(wu_h.at[:, cols], wgu.at[t, 1], wsem.at[t // 2]),
        )

    @pl.loop(0, T)
    def _(t):
        for c in wload(t):
            c.start()

    for c in loads[4:]:
        c.start()

    for part, m in ((0, 4), (1, 12)):
        i = lax.broadcasted_iota(jnp.int32, (16 * m, 16 * m), 0)
        j = lax.broadcasted_iota(jnp.int32, (16 * m, 16 * m), 1)
        y, z = (j >> 1) & 3, (j >> 3) & 3
        rest_of = (j >> 6) * 4 + ((j >> 5) & 1) * 2 + (j & 1)
        for order, (u, v) in enumerate(((y, z), (z, y))):
            perm[part][order] = jnp.where(i == u * (4 * m) + v * m + rest_of, 1.0, 0.0).astype(BF16)
    i = lax.broadcasted_iota(jnp.int32, (64, 64), 0)
    j = lax.broadcasted_iota(jnp.int32, (64, 64), 1)
    k, q = i >> 4, i & 15
    join[...] = jnp.where(j == jnp.where(q < 4, k * 4 + q, 12 + k * 12 + q), 1.0, 0.0).astype(BF16)
    vb[0][...] = jnp.zeros_like(vb[0])
    vb[1][...] = jnp.zeros_like(vb[1])

    take(ybuf.at[0:3], d_rs.at[0])

    def zcols(zd):
        return pl.ds(pl.multiple_of(zd * K, 128), K)

    second = [
        pltpu.make_async_remote_copy(
            ybuf.at[:, :, zcols(h.at("z", k))], zbuf.at[h.z], d_ss.at[1], d_rs.at[k],
            device_id=h.dev("z", k), device_id_type=MESH)
        for k in (2, 1, 3)
    ]
    for c in second:
        c.start()

    def along(k, flip):
        return lax.rem(h.x + k, 4) * 2 + lax.rem(h.c + flip, 2)

    def to_x(n, k, flip):
        z, slot = h.at("z", n), (4 - k) % 4
        return pltpu.make_async_remote_copy(
            xr.at[h.c, z], xr.at[slot * 2 + h.c, z], d_ss.at[2], d_rs.at[4 if k == 0 else 5],
            device_id=(h.gx, along(k, flip)), device_id_type=MESH)

    for n in (0, 1, 3, 2):
        z = h.at("z", n)
        if n == 0:
            for y in range(4):
                a8[n, 2 * y:2 * y + 2, :] = f32(ybuf[y, :, zcols(h.z)])
        else:
            second[{2: 0, 1: 1, 3: 2}[4 - n]].wait_recv()
            for y in range(4):
                a8[n, 2 * y:2 * y + 2, :] = f32(zbuf[z, y])
        xr[h.c, z] = a8[n].astype(BF16)
        for k, flip in ((0, 1), (3, 0), (3, 1), (2, 0), (2, 1), (1, 0), (1, 1)):
            to_x(n, k, flip).start()

    def rows(part):
        take(xr.at[0:(1, 6)[part]], d_rs.at[4 + part])
        for n in range(3):
            cols = slice(n * 384, (n + 1) * 384)
            got = xr[0:2, :, :, cols].reshape(64, 384) if part == 0 else xr[2:8, :, :, cols].reshape(192, 384)
            for order in (0, 1):
                xs[part][order, :, cols] = jnp.dot(
                    perm[part][order], got, preferred_element_type=F32).astype(BF16)

    def stream_of(b, lead, n, first, s, ss, rs):
        at = lead + (n,)
        return Stream(
            h, first, s, [b[0].at[at], b[1].at[at]], b[2].at[at], [r.at[at] for r in b[3:6]],
            [r.at[lead + (0, n)] for r in b[6:9]], [r.at[lead + (1, n)] for r in b[6:9]], tmp, ss, rs)

    att = [
        stream_of(qb, (), n, first, s, q_ss, q_rs)
        for n, (first, s) in enumerate([("y", -1), ("y", 1), ("z", 1)])
    ]
    att.append(stream_of(vb, (), 0, "z", -1, v_ss, v_rs))

    def att_take(ph, role):
        for b, sem in ((qb, q_rs), (vb, v_rs)):
            take(b[3 + 3 * role + ph], sem.at[ph * 2 + role])

    def pair_take(i, ph, role):
        take(fb[3 + 3 * role + ph].at[pl.ds(2 * i, 2)], f_rs.at[i, ph * 2 + role])

    def pair(i, do):
        for t, order in ((2 * i, "y"), (2 * i + 1, "z")):
            do(t, [stream_of(fb, (t,), n, order, -1 if n == 0 else 1, f_ss, f_rs.at[i]) for n in (0, 1)])

    def query(part):
        m = (16, 48)[part]
        val = jnp.dot(xs[part][0], wq[:, :2 * DH], preferred_element_type=F32)
        for n in range(2):
            qb[part][n] = val[:, n * DH:(n + 1) * DH].reshape(4, m, DH)
        qb[part][2] = jnp.dot(xs[part][1], wq[:, 2 * DH:], preferred_element_type=F32).reshape(4, m, DH)
        vb[part][0, :, :, 0:64] = lax.dot_general(
            xs[part][1], wkv[...], (((1,), (1,)), ((), ())), preferred_element_type=F32
        ).reshape(4, m, 64)
        for s in att:
            s.start(part)

    def computes(part, lo, hi):
        @pl.loop(lo, hi)
        def _(i):
            if part == 0:
                blocks = wgu.at[pl.ds(2 * i, 2)]
                pltpu.make_async_copy(blocks, blocks, wsem.at[i]).wait()
            for order in (0, 1):
                t = 2 * i + order
                for n in (0, 1):
                    val = jnp.dot(xs[part][order], wgu[t, n], preferred_element_type=F32)
                    fb[part][t, n] = val.astype(BF16).reshape(4, (16, 48)[part], W)
            pair(i, lambda t, ss: [s.start(part) for s in ss])

    def relays(ph, lo, hi):
        @pl.loop(lo, hi)
        def _(i):
            pair_take(i, ph, 0)
            pair(i, lambda t, ss: [s.relay(ph) for s in ss])

    def turns(lo, hi, direct):
        @pl.loop(lo, hi)
        def _(i):
            for ph in (0, 1):
                pair_take(i, ph, 1)
            group = []
            pair(i, lambda t, ss: group.extend(ss))
            for n, s in enumerate(group):
                cols = slice(n * W, (n + 1) * W)
                both[0:16, cols] = s.total(0).astype(BF16)
                both[16:64, cols] = s.total(1).astype(BF16)
            for n, s in enumerate(group):
                val = jnp.dot(join[...], both[:, n * W:(n + 1) * W], preferred_element_type=F32)
                s.mid[...] = val.astype(BF16).reshape(4, 16, W)
            for s in group:
                s.start(2, direct)

    def att_relay(ph):
        att_take(ph, 0)
        for s in att:
            s.relay(ph)

    rows(0)
    loads[2].wait()
    loads[3].wait()
    query(0)
    computes(0, 0, T // 2)
    rows(1)
    query(1)
    att_relay(0)
    relays(0, 0, 4)
    computes(1, 0, 2)
    relays(0, 4, T // 2)
    computes(1, 2, 4)
    att_relay(1)
    computes(1, 4, T // 2)
    relays(1, 0, 3)
    relays(1, 3, T // 2)
    for ph in (0, 1):
        att_take(ph, 1)
    for s in att:
        s.turn(True)
    turns(0, DIRECT, False)

    turns(DIRECT, T // 2, True)

    att_take(2, 0)
    att_take(2, 1)
    for n, s in enumerate(att):
        val = s.total(2, True)
        for g in range(8):
            qs[g, :, n * DH:n * DH + val.shape[1]] = val[2 * g:2 * g + 2, :].astype(BF16)
    give = [
        pltpu.make_async_remote_copy(
            qs.at[2 * k + lax.rem(h.c + flip, 2)], qr.at[h.gy], g_ss.at[0], g_rs.at[0],
            device_id=(h.gx, along(k, flip)), device_id_type=MESH)
        for k in range(4) for flip in (0, 1) if k or flip
    ]
    for c in give:
        c.start()
    qr[h.gy] = qs[h.c]
    relays(2, 0, DIRECT)

    take(qr.at[0:7], g_rs.at[0])
    for g in range(8):
        for n in range(3):
            row = f32(qr[g, :, n * DH:(n + 1) * DH])
            for r in range(2):
                qa[r, g * 3 + n:g * 3 + n + 1, :] = row[r:r + 1, :]
        kvs[2 * g:2 * g + 2, :] = f32(qr[g, :, 768:896])
    moved = pltpu.roll(kvs[...], 64, axis=1)

    def whole(r, first):
        row = [(kvs[2 * g + r:2 * g + r + 1, :], moved[2 * g + r:2 * g + r + 1, :]) for g in range(first, first + 4)]
        return jnp.concatenate([row[0][0] + row[1][1], row[2][0] + row[3][1]], axis=1)

    for c in loads[4:]:
        c.wait()
    scale = DH ** (-0.5)
    for r in range(2):
        query = qa[r]
        scores = lax.dot_general(
            query.astype(BF16), kc[r], (((1,), (1,)), ((), ())), preferred_element_type=F32) * scale
        score_new = jnp.sum(query * whole(r, 0), axis=1, keepdims=True) * scale
        mask = lax.broadcasted_iota(jnp.int32, (HEADS, CACHE), 1) < lengths[r]
        top = jnp.maximum(jnp.max(jnp.where(mask, scores, -1e30), axis=1, keepdims=True), score_new)
        exponent = jnp.where(mask, jnp.exp(scores - top), 0.0)
        exponent_new = jnp.exp(score_new - top)
        total = jnp.sum(exponent, axis=1, keepdims=True) + exponent_new
        weights = (exponent / total).astype(BF16)
        weights_new = f32((exponent_new / total).astype(BF16))
        out = jnp.dot(weights, vc[r], preferred_element_type=F32) + weights_new * whole(r, 4)
        for n in range(HEADS):
            context[r:r + 1, n * DH:(n + 1) * DH] = out[n:n + 1, :].astype(BF16)

    def finish(direct, t, ss):
        gate, up = (s.total(2, direct) for s in ss)
        cols = pl.ds(pl.multiple_of(t * W, 128), W)
        val = gate / (1.0 + jnp.exp(-gate)) * up
        val = jnp.where(h.x % 2 == 1, jnp.roll(val, 4, axis=0), val)
        val = jnp.where(h.x >= 2, jnp.roll(val, 8, axis=0), val)
        hidden[:, cols] = val.astype(BF16)

    @pl.loop(0, DIRECT)
    def _(i):
        pair_take(i, 2, 1)
        pair(i, functools.partial(finish, False))

    @pl.loop(DIRECT, T // 2)
    def _(i):
        pair_take(i, 2, 0)
        pair_take(i, 2, 1)
        pair(i, functools.partial(finish, True))

    sent(ybuf.at[0:3], d_ss.at[0])
    sent(zbuf.at[0:3], d_ss.at[1])
    sent(xr.at[0:7], d_ss.at[2])
    sent(qr.at[0:7], g_ss.at[0])
    for b, ss in ((fb, f_ss), (qb, q_ss), (vb, v_ss)):
        for ph in range(3):
            for i in range(3):
                sent(b[3 + ph], ss.at[ph * 3 + i])


def fused(stream, gain, w_gate, w_up, w_query, w_keyval, k_cache, v_cache, lengths):
    vm, dma = pltpu.VMEM, pltpu.SemaphoreType.DMA

    def rs(lead, wide, kind):
        ms = (16, 48, 16)
        return [
            *[vm(lead + (4, m, wide), kind) for m in ms],
            *[vm(lead + (m, wide), kind) for m in ms],
            *[vm(lead[:-1] + (2,) + lead[-1:] + (m, wide), kind) for m in ms],
        ]

    return pl.pallas_call(
        kernel,
        out_shape=(
            vm((16, FF), BF16),
            vm((2, HEADS * DH), BF16),
        ),
        in_specs=[pl.BlockSpec(memory_space=pl.ANY)] * 9,
        out_specs=[pl.BlockSpec(memory_space=pltpu.VMEM)] * 2,
        scratch_shapes=[
            vm((2, D), BF16), vm((1, D), F32), vm((T, 2, K, W), BF16),
            vm((K, 768), BF16), vm((64, K), BF16), vm((2, CACHE, DH), BF16), vm((2, CACHE, DH), BF16),
            pltpu.SMEM((2,), jnp.int32), dma((7,)), dma((T // 2,)),
            vm((4, 2, 4 * K), BF16), vm((4, 2, 4 * K), BF16), vm((4, 4, 2, K), BF16), vm((4, 8, K), F32),
            vm((8, 4, 8, K), BF16), vm((2, 64, 64), BF16), vm((2, 192, 192), BF16),
            vm((2, 64, K), BF16), vm((2, 192, K), BF16), vm((4, 16, W), F32),
            vm((64, 4 * W), BF16), vm((64, 64), BF16),
            dma((3,)), dma((6,)),
            *rs((T, 2), W, BF16), *rs((3,), DH, F32), *rs((1,), 128, F32),
            dma((9,)), dma((T // 2, 6)), dma((9,)), dma((6,)), dma((9,)), dma((6,)),
            vm((8, 2, 896), BF16), vm((8, 2, 896), BF16), vm((2, HEADS, DH), F32), vm((16, 128), F32),
            dma((1,)), dma((1,)),
        ],
        compiler_params=pltpu.CompilerParams(
            collective_id=0, has_side_effects=True, vmem_limit_bytes=62 * 2**20
        ),
    )(stream, gain, w_gate, w_up, w_query, w_keyval, k_cache, v_cache, lengths)


def write(hidden, context, hidden_h, context_h, sem):
    copies = [
        pltpu.make_async_copy(hidden, hidden_h, sem.at[0]),
        pltpu.make_async_copy(context, context_h, sem.at[1]),
    ]
    for c in copies:
        c.start()
    for c in copies:
        c.wait()


def body(stream, norm_gain, w_gate, w_up, w_query, w_keyval, k_cache, v_cache, lengths):
    hidden, context = fused(
        stream, norm_gain.reshape(1, D), w_gate, w_up, w_query, w_keyval.T, k_cache, v_cache, lengths
    )
    return pl.pallas_call(
        write,
        out_shape=(
            jax.ShapeDtypeStruct((16, FF), BF16),
            jax.ShapeDtypeStruct((2, HEADS * DH), BF16),
        ),
        in_specs=[pl.BlockSpec(memory_space=pl.ANY)] * 2,
        out_specs=[pl.BlockSpec(memory_space=pl.ANY)] * 2,
        scratch_shapes=[pltpu.SemaphoreType.DMA((2,))],
    )(*(pltpu.with_memory_space_constraint(v, pltpu.VMEM) for v in (hidden, context)))


def solution(mesh):
    return jax.shard_map(
        body,
        mesh=mesh,
        in_specs=(
            P(("gx", "gy"), None),
            P(),
            P("gx", "gy"),
            P("gx", "gy"),
            P("gx", "gy"),
            P("gx", "gy"),
            P(("gx", "gy"), None, None),
            P(("gx", "gy"), None, None),
            P(("gx", "gy")),
        ),
        out_specs=(P("gx", "gy"), P(("gx", "gy"), None)),
        check_vma=False,
    )
```
